32 devices in a mesh: dp: 32 (over z, y, x, core).
Axes of the slice: x: 2, y: 2, z: 4, core: 2. Of those that a mesh axis runs over, the one named last changes fastest.
Arguments:
- tokens: bfloat16 [6144, 768], P('dp'), may hold values from -6 to 6
- seq_ids: int32 [6144], P('dp'), may hold values from -1 to 1, as said below
- positions: int32 [6144], P('dp'), may hold values from 0 to 191, as said below
- cotangent: bfloat16 [6144, 768], P('dp'), may hold values from -6 to 6
- attn_gain: bfloat16 [768], P('dp'), may hold values from 0.099609375 to 1.8984375
- w_query: bfloat16 [768, 768], P('dp'), may hold values from -0.21875 to 0.21875
- w_key: bfloat16 [768, 768], P('dp'), may hold values from -0.21875 to 0.21875
- w_value: bfloat16 [768, 768], P('dp'), may hold values from -0.21875 to 0.21875
- w_output: bfloat16 [768, 768], P(None, 'dp'), may hold values from -0.875 to 0.875
- mlp_gain: bfloat16 [768], P('dp'), may hold values from 0.099609375 to 1.8984375
- w_gate: bfloat16 [768, 3072], P('dp'), may hold values from -0.21875 to 0.21875
- w_up: bfloat16 [768, 3072], P('dp'), may hold values from -0.21875 to 0.21875
- w_down: bfloat16 [3072, 768], P(None, 'dp'), may hold values from -0.109375 to 0.109375
Outputs:
- out: bfloat16 [6144, 768], P('dp')
- d_tokens: bfloat16 [6144, 768], P('dp')
- d_attn_gain: float32 [768], P('dp')
- d_w_query: float32 [768, 768], P('dp')
- d_w_key: float32 [768, 768], P('dp')
- d_w_value: float32 [768, 768], P('dp')
- d_w_output: float32 [768, 768], P(None, 'dp')
- d_mlp_gain: float32 [768], P('dp')
- d_w_gate: float32 [768, 3072], P('dp')
- d_w_up: float32 [768, 3072], P('dp')
- d_w_down: float32 [3072, 768], P(None, 'dp')
The draws below stay inside these ranges and needn't reach their ends.
Inputs may be any that keep to these rules, and one draw needn't show every extreme that they name: `seq_ids`: in each aligned block of 192 slots (the slots of one device) the live slots come first: sequence 0, then possibly sequence 1, then empty slots (-1). Each sequence has at least 24 slots, each block at least 96 live slots, and some block is entirely live. `positions`: A token's position counts from 0 at its sequence's first slot and rises by one a slot; empty slots hold 0.
All inputs are finite; a program needn't handle non-finite values.
Results may differ from the reference program's by a relative error of at most 0.013.
Values may be sent and summed in bfloat16 or wider, within the bound.
No kernel may reach another device: no remote copies, remote signals or barrier semaphores. Data moves between devices by JAX's collectives and lax.ppermute only.
A program may use at most 128 MiB of HBM per device.

```python
import math
import jax
import jax.numpy as jnp
from jax import lax

D = 768
H = 12
KVH = 12
HD = 64
FF = 3072
TOK_DEV = 192
TOKENS = 6144


def segment_layout(key):
    devices = TOKENS // TOK_DEV
    key_full, key_live, key_count, key_cut = jax.random.split(jax.random.fold_in(key, 7), 4)
    device_full = jax.random.randint(key_full, (), 0, devices)
    device_half = (device_full + 1) % devices
    device_index = jnp.arange(devices, dtype=jnp.int32)
    live_count = jax.random.randint(key_live, (devices,), TOK_DEV // 2, TOK_DEV + 1)
    live_count = jnp.where(device_index == device_full, TOK_DEV, jnp.where(device_index == device_half, TOK_DEV // 2, live_count))
    two_seqs = jax.random.randint(key_count, (devices,), 0, 2)
    two_seqs = jnp.where(device_index == device_full, 0, jnp.where(device_index == device_half, 1, two_seqs))
    cut_point = jax.random.randint(key_cut, (devices,), live_count // 4, live_count - live_count // 4 + 1)
    cut_point = jnp.where(two_seqs == 1, cut_point, live_count)
    slot_index = jnp.arange(TOK_DEV, dtype=jnp.int32)[None, :]
    first_seq = slot_index < cut_point[:, None]
    is_live = slot_index < live_count[:, None]
    seg_table = jnp.where(first_seq, 0, jnp.where(is_live, 1, -1)).astype(jnp.int32)
    pos_table = jnp.where(first_seq, slot_index, jnp.where(is_live, slot_index - cut_point[:, None], 0)).astype(jnp.int32)
    return (seg_table.reshape(-1), pos_table.reshape(-1))


def draw_seq_ids(key, part):
    return segment_layout(key)[0]


def draw_positions(key, part):
    return segment_layout(key)[1]


def with_spikes(values, rng, source, target, shards_of, factor):
    owner, partner = [(jnp.arange(values.shape[axis_at]) // (values.shape[axis_at] // shards_of)).reshape([-1 if axis == axis_at else 1 for axis in range(values.ndim)]) for axis_at in (source, target)]
    chosen = jax.random.permutation(rng, shards_of)[partner]
    strong = (owner == chosen) | (owner == (partner + shards_of // 2) % shards_of)
    return jnp.where(strong, factor * values, values)


def block_scale(key, dims, cuts, least, top_value):
    loudness, own = 1.0, jax.random.fold_in(key, 6)
    for position, blocks in cuts:
        draws = jnp.exp(jax.random.uniform(jax.random.fold_in(own, position), (blocks,), jnp.float32, least / len(cuts), top_value / len(cuts)))
        loudness = loudness * jnp.repeat(draws, dims[position] // blocks).reshape([-1 if axis == position else 1 for axis in range(len(dims))])
    return loudness


def noise(own_key, shape, scale, bound, cuts=(), kind=jnp.bfloat16):
    values = scale * jax.random.normal(own_key, shape, jnp.float32)
    if cuts:
        values = values * block_scale(own_key, shape, cuts, -0.22, 0.18)
    return jnp.clip(values, -bound, bound).astype(kind)


def noise_with(key, dims, width, limit, cuts, heavy, kind=jnp.bfloat16):
    entries = width * jax.random.normal(key, dims, jnp.float32)
    if cuts:
        entries = entries * block_scale(key, dims, cuts, -0.22, 0.18)
    return jnp.clip(with_spikes(entries, jax.random.fold_in(key, 3), *heavy), -limit, limit).astype(kind)


def setup_inputs(seed: int = 0) -> dict:
    keys = jax.random.split(jax.random.key(seed), 14)
    tokens = noise_with(keys[0], (TOKENS, D), 1.0, 6.0, ((0, 32),), (0, 1, 32, 2.75))
    seq_ids = draw_seq_ids(jax.random.fold_in(keys[13], 71), 0)
    positions = draw_positions(jax.random.fold_in(keys[13], 71), 0)
    cotangent = noise_with(keys[3], (TOKENS, D), 1.0, 6.0, ((0, 32),), (0, 1, 32, 2.75))
    attn_gain = jnp.clip(1.0 + 0.18 * jax.random.normal(keys[4], (D,), jnp.float32), 0.099609375, 1.8984375).astype(jnp.bfloat16)
    w_query = noise(keys[5], (D, D), D ** -0.5, 0.21875, ((0, 32),))
    w_key = noise(keys[6], (D, KVH * HD), D ** -0.5, 0.21875, ((0, 32),))
    w_value = noise(keys[7], (D, KVH * HD), D ** -0.5, 0.21875, ((0, 32),))
    w_output = noise(keys[8], (D, D), (D // 16) ** -0.5, 0.875, ((1, 32),))
    mlp_gain = jnp.clip(1.0 + 0.18 * jax.random.normal(keys[9], (D,), jnp.float32), 0.099609375, 1.8984375).astype(jnp.bfloat16)
    w_gate = noise(keys[10], (D, FF), D ** -0.5, 0.21875, ((0, 32),))
    w_up = noise(keys[11], (D, FF), D ** -0.5, 0.21875, ((0, 32),))
    w_down = noise(keys[12], (FF, D), FF ** -0.5, 0.109375, ((1, 32),))
    return dict(tokens=tokens, seq_ids=seq_ids, positions=positions, cotangent=cotangent, attn_gain=attn_gain, w_query=w_query, w_key=w_key, w_value=w_value, w_output=w_output, mlp_gain=mlp_gain, w_gate=w_gate, w_up=w_up, w_down=w_down)


@jax.custom_vjp
def low(v):
    return lax.optimization_barrier(v.astype(jnp.bfloat16)).astype(jnp.float32)

@jax.custom_vjp
def low_back(v):
    return v

def low_keep(v):
    return (low(v), None)

def low_pass(kept, grad):
    return (grad,)

def back_keep(v):
    return (v, None)

def back_low(kept, grad):
    return (low(grad),)
low.defvjp(low_keep, low_pass)
low_back.defvjp(back_keep, back_low)
epsilon = 1e-05
masked_value = -1e+30
theta_base = 10000.0
highest = lax.Precision.HIGHEST

def rotation(positions, head_size):
    half_size = head_size // 2
    frequency = jnp.exp(jnp.arange(half_size, dtype=jnp.float32) * (-2.0 * math.log(theta_base) / head_size))
    angles = positions.astype(jnp.float32)[:, None] * frequency[None, :]
    return (jnp.cos(angles)[:, None, :], jnp.sin(angles)[:, None, :])

def rotate(values, cosine, sine_part):
    half_size = values.shape[-1] // 2
    first_half = values[..., :half_size]
    second_half = values[..., half_size:]
    return jnp.concatenate([first_half * cosine - second_half * sine_part, second_half * cosine + first_half * sine_part], axis=-1)

def allowed(seg_rows, seg_keys, row_start):
    row_index = row_start + jnp.arange(seg_rows.shape[0], dtype=jnp.int32)
    key_index = jnp.arange(seg_keys.shape[0], dtype=jnp.int32)
    same_seq = (seg_rows[:, None] == seg_keys[None, :]) & (seg_rows[:, None] >= 0) & (key_index[None, :] <= row_index[:, None])
    return same_seq | (key_index[None, :] == row_index[:, None])

def attend(inputs):
    query_block, key_block, value_block, seg_block = inputs
    scores = low_back(jnp.einsum('qhgd,khd->hgqk', query_block, key_block, precision=highest))
    allowed_mask = allowed(seg_block, seg_block, 0)
    logits = jnp.where(allowed_mask[None, None], scores * HD ** (-0.5), masked_value)
    row_top = lax.optimization_barrier(jnp.max(logits, axis=-1, keepdims=True))
    exponent = jnp.exp(logits - row_top)
    softmax_weights = low(exponent / lax.optimization_barrier(jnp.sum(exponent, axis=-1, keepdims=True)))
    mixed_heads = jnp.einsum('hgqk,khd->qhgd', softmax_weights, value_block, precision=highest)
    return mixed_heads.reshape(mixed_heads.shape[0], H * HD)

def matmul(left, right):
    return jnp.dot(left, right, precision=highest, preferred_element_type=jnp.float32)

def reference(tokens, seq_ids, positions, cotangent, attn_gain, w_query, w_key, w_value, w_output, mlp_gain, w_gate, w_up, w_down):
    cosine, sine_part = rotation(positions, HD)
    blocks = TOKENS // TOK_DEV
    groups = H // KVH
    live_rows = (seq_ids >= 0).astype(jnp.float32)

    def forward(stream, gain_one, query_w, key_w, value_w, output_w, gain_two, gate_w, up_w, down_w):
        scale_one = lax.rsqrt(lax.optimization_barrier(jnp.mean(stream * stream, axis=-1, keepdims=True)) + epsilon)
        normed_one = low(stream * scale_one * gain_one)
        queries = low_back(matmul(normed_one, query_w))
        keys_proj = low_back(matmul(normed_one, key_w))
        values_proj = low(low_back(matmul(normed_one, value_w)))
        queries_rot = low(rotate(queries.reshape(TOKENS, H, HD), cosine, sine_part))
        keys_rot = low(rotate(keys_proj.reshape(TOKENS, KVH, HD), cosine, sine_part))
        heads_out = lax.map(jax.checkpoint(attend), (queries_rot.reshape(blocks, TOK_DEV, KVH, groups, HD), keys_rot.reshape(blocks, TOK_DEV, KVH, HD), values_proj.reshape(blocks, TOK_DEV, KVH, HD), seq_ids.reshape(blocks, TOK_DEV)))
        heads_low = low(low_back(heads_out.reshape(TOKENS, H * HD)))
        middle = stream + low_back(matmul(heads_low, output_w))
        scale_two = lax.rsqrt(lax.optimization_barrier(jnp.mean(middle * middle, axis=-1, keepdims=True)) + epsilon)
        normed_two = low(middle * scale_two * gain_two)
        gate_val = low_back(matmul(normed_two, gate_w))
        up_val = low_back(matmul(normed_two, up_w))
        activ = low(jax.nn.silu(gate_val) * up_val)
        return middle + low_back(matmul(activ, down_w))
    params = tuple((weight_in.astype(jnp.float32) for weight_in in (tokens, attn_gain, w_query, w_key, w_value, w_output, mlp_gain, w_gate, w_up, w_down)))
    result, pullback = jax.vjp(forward, *params)
    grads = pullback(cotangent.astype(jnp.float32) * live_rows[:, None])
    return (result.astype(jnp.bfloat16), grads[0].astype(jnp.bfloat16), grads[1], grads[2], grads[3], grads[4], grads[5], grads[6], grads[7], grads[8], grads[9])
```

```python
import math

import jax
import jax.numpy as jnp
from jax import lax
from jax.sharding import PartitionSpec as P

H = 12
HD = 64
FF_CHUNKS = 4
EPS = 1e-05
MASKED = -1e30
THETA = 10000.0


f32 = jnp.float32
bf16 = jnp.bfloat16


def gather_orders(n):
    if n == 32:
        return (16, 2, 8, 4, 1), (16, 4, 8, 2, 1)
    bits = [1 << k for k in range(n.bit_length() - 1)]
    order = tuple(reversed(bits))
    return order, order


def nn(a, b):
    return jnp.dot(a, b, preferred_element_type=f32)


def nt(a, b):
    return lax.dot_general(a, b, (((1,), (1,)), ((), ())), preferred_element_type=f32)


def tn(a, b):
    return lax.dot_general(a, b, (((0,), (0,)), ((), ())), preferred_element_type=f32)


def rotate(v, cosine, sine):
    half = v.shape[-1] // 2
    a, b = v[..., :half], v[..., half:]
    return jnp.concatenate([a * cosine - b * sine, b * cosine + a * sine], axis=-1)


def rotate_back(v, cosine, sine):
    half = v.shape[-1] // 2
    a, b = v[..., :half], v[..., half:]
    return jnp.concatenate([a * cosine + b * sine, b * cosine - a * sine], axis=-1)


def make_on_device(n):
    first, second = gather_orders(n)
    axis_bits = tuple(reversed(first))
    axis_of = {b: i for i, b in enumerate(axis_bits)}
    k = len(axis_bits)

    def swap(a, b):
        return lax.ppermute(a, "dp", [(i, i ^ b) for i in range(n)])

    def gather(shard, order):
        a = shard.reshape((1,) * k + shard.shape)
        for b in order:
            a = jnp.concatenate([a, swap(a, b)], axis=axis_of[b])
        return a.reshape((n * shard.shape[0],) + shard.shape[1:])

    def scatter(g, order):
        rows = g.shape[0] // n
        a = g.reshape((2,) * k + (rows,) + g.shape[1:])
        for i, b in enumerate(reversed(order)):
            keep = lax.slice_in_dim(a, 0, 1, axis=axis_of[b])
            send = lax.slice_in_dim(a, 1, 2, axis=axis_of[b])
            a = keep.astype(f32) + swap(send, b).astype(f32)
            if i < k - 1:
                a = a.astype(bf16)
        return a.reshape((rows,) + g.shape[1:])

    def on_device(tokens, seq_ids, positions, cotangent, attn_gain, w_query, w_key, w_value, w_output,
                  mlp_gain, w_gate, w_up, w_down):
        toks, d = tokens.shape
        rows = d // n
        ff = w_gate.shape[1]
        fc = ff // FF_CHUNKS
        gains = jnp.stack([attn_gain, mlp_gain], axis=1)
        gains = jnp.pad(gains, ((0, 0), (0, 126)))
        wq = gather(jnp.concatenate([w_query, gains], axis=1), first)
        wk = gather(w_key, second)
        wv = gather(w_value, first)
        wo = gather(w_output.T, second)
        down_t = w_down.T
        wff = []
        for j in range(FF_CHUNKS):
            cut = slice(j * fc, (j + 1) * fc)
            part = jnp.concatenate([w_gate[:, cut], w_up[:, cut], down_t[:, cut]], axis=1)
            wff.append(gather(part, (first, second)[j % 2]))
        gain_one = wq[:, d].astype(f32)
        gain_two = wq[:, d + 1].astype(f32)
        wq = wq[:, :d]
        me = lax.axis_index("dp")
        slot = jnp.arange(d, dtype=jnp.int32) // rows
        owner = jnp.zeros_like(slot)
        for i, b in enumerate(axis_bits):
            owner = owner + ((slot >> (k - 1 - i)) & 1) * b
        source = (owner ^ me) * rows + jnp.arange(d, dtype=jnp.int32) % rows
        select = (jnp.arange(d, dtype=jnp.int32)[:, None] == source[None, :]).astype(bf16)
        live = (seq_ids >= 0).astype(f32)[:, None]
        x = nn(tokens, select)
        g = nn(cotangent, select) * live
        freq = jnp.exp(jnp.arange(HD // 2, dtype=f32) * (-2.0 * math.log(THETA) / HD))
        angles = positions.astype(f32)[:, None] * freq[None, :]
        cosine, sine = jnp.cos(angles)[:, None, :], jnp.sin(angles)[:, None, :]
        index = jnp.arange(toks, dtype=jnp.int32)
        allowed = (seq_ids[:, None] == seq_ids[None, :]) & (seq_ids[:, None] >= 0) & (index[None, :] <= index[:, None])
        allowed = (allowed | (index[None, :] == index[:, None]))[None]
        scale = HD ** -0.5
        r1 = lax.rsqrt(jnp.mean(x * x, axis=-1, keepdims=True) + EPS)
        n1 = (x * r1 * gain_one).astype(bf16)
        heads = lambda v: v.reshape(toks, H, HD)
        qr = rotate(heads(nn(n1, wq)), cosine, sine).astype(bf16)
        kr = rotate(heads(nn(n1, wk)), cosine, sine).astype(bf16)
        vb = heads(nn(n1, wv).astype(bf16))
        s = jnp.einsum("qhd,khd->hqk", qr, kr, preferred_element_type=f32)
        logits = jnp.where(allowed, s * scale, MASKED)
        e = jnp.exp(logits - jnp.max(logits, axis=-1, keepdims=True))
        p = e / jnp.sum(e, axis=-1, keepdims=True)
        pb = p.astype(bf16)
        ob = jnp.einsum("hqk,khd->qhd", pb, vb, preferred_element_type=f32).astype(bf16).reshape(toks, d)
        hmid = x + nt(ob, wo)
        r2 = lax.rsqrt(jnp.mean(hmid * hmid, axis=-1, keepdims=True) + EPS)
        n2 = (hmid * r2 * gain_two).astype(bf16)
        gb = g.astype(bf16)
        y = hmid
        dn2 = jnp.zeros_like(hmid)
        d_ff = []
        for j in range(FF_CHUNKS):
            w = wff[j]
            gate_up = nn(n2, w[:, : 2 * fc])
            gate, up = gate_up[:, :fc], gate_up[:, fc:]
            sig = jax.nn.sigmoid(gate)
            silu = gate * sig
            act = (silu * up).astype(bf16)
            y = y + nt(act, w[:, 2 * fc :])
            dact = nn(gb, w[:, 2 * fc :])
            dgate = (dact * up * sig * (1.0 + gate * (1.0 - sig))).astype(bf16)
            dup = (dact * silu).astype(bf16)
            both = jnp.concatenate([dgate, dup], axis=1)
            dn2 = dn2 + nt(both, w[:, : 2 * fc])
            dw = jnp.concatenate([tn(n2, both).astype(bf16), tn(gb, act).astype(bf16)], axis=1)
            d_ff.append(scatter(dw, (first, second)[j % 2]))
        d_gain_two = jnp.sum(dn2 * hmid * r2, axis=0)
        t2 = dn2 * gain_two
        dh = g + r2 * t2 - hmid * r2 ** 3 * jnp.mean(t2 * hmid, axis=-1, keepdims=True)
        dhb = dh.astype(bf16)
        d_wo = scatter(tn(dhb, ob).astype(bf16), first)
        dob = heads(nn(dhb, wo).astype(bf16))
        dp = jnp.einsum("qhd,khd->hqk", dob, vb, preferred_element_type=f32)
        dlogit = p * (dp - jnp.sum(dp * p, axis=-1, keepdims=True))
        ds = (jnp.where(allowed, dlogit, 0.0) * scale).astype(bf16)
        dv = jnp.einsum("hqk,qhd->khd", pb, dob, preferred_element_type=f32).astype(bf16).reshape(toks, d)
        d_wv = scatter(tn(n1, dv).astype(bf16), second)
        dqr = jnp.einsum("hqk,khd->qhd", ds, kr, preferred_element_type=f32)
        dkr = jnp.einsum("hqk,qhd->khd", ds, qr, preferred_element_type=f32)
        dq = rotate_back(dqr, cosine, sine).astype(bf16).reshape(toks, d)
        dk = rotate_back(dkr, cosine, sine).astype(bf16).reshape(toks, d)
        d_wq = scatter(tn(n1, dq).astype(bf16), first)
        dn1 = nt(dq, wq) + nt(dk, wk) + nt(dv, wv)
        d_gain_one = jnp.sum(dn1 * x * r1, axis=0)
        t1 = dn1 * gain_one
        d_tokens = dh + r1 * t1 - x * r1 ** 3 * jnp.mean(t1 * x, axis=-1, keepdims=True)
        d_gains = jnp.pad(jnp.stack([d_gain_one, d_gain_two], axis=1), ((0, 0), (0, 126))).astype(bf16)
        d_wk = scatter(jnp.concatenate([tn(n1, dk).astype(bf16), d_gains], axis=1), second)
        d_gate = jnp.concatenate([c[:, :fc] for c in d_ff], axis=1)
        d_up = jnp.concatenate([c[:, fc : 2 * fc] for c in d_ff], axis=1)
        d_down = jnp.concatenate([c[:, 2 * fc :] for c in d_ff], axis=1)
        back = lambda v: nt(v.astype(bf16), select).astype(bf16)
        return (back(y), back(d_tokens), d_wk[:, d], d_wq, d_wk[:, :d], d_wv, d_wo.T, d_wk[:, d + 1],
                d_gate, d_up, d_down.T)

    return on_device


def solution(mesh):
    rows, cols, vec = P("dp", None), P(None, "dp"), P("dp")
    in_specs = (rows, vec, vec, rows, vec, rows, rows, rows, cols, vec, rows, rows, cols)
    out_specs = (rows, rows, vec, rows, rows, rows, cols, vec, rows, rows, cols)
    return jax.shard_map(make_on_device(mesh.shape["dp"]), mesh=mesh, in_specs=in_specs, out_specs=out_specs, check_vma=False)
```

```python
import math

import jax
import jax.numpy as jnp
from jax import lax
from jax.experimental import pallas as pl
from jax.experimental.pallas import tpu as pltpu
from jax.sharding import PartitionSpec as P

HD = 64
LOW = (2, 1)
PARTS = 2
EPS = 1e-05
MASKED = -1e30
THETA = 10000.0


f32 = jnp.float32
bf16 = jnp.bfloat16


def gather_orders(n):
    if n == 32:
        return (16, 2, 8, 4, 1), (16, 4, 8, 2, 1)
    bits = [1 << k for k in range(n.bit_length() - 1)]
    order = tuple(reversed(bits))
    return order, order


def nn(a, b):
    return jnp.dot(a, b, preferred_element_type=f32)


def nt(a, b):
    return lax.dot_general(a, b, (((1,), (1,)), ((), ())), preferred_element_type=f32)


def call(kernel, outs, *args, **kw):
    out_shape = [jax.ShapeDtypeStruct(s, d) for s, d in outs]
    vmem = pl.BlockSpec(memory_space=pltpu.VMEM)
    return pl.pallas_call(
        kernel, out_shape=out_shape, in_specs=[vmem] * len(args), out_specs=[vmem] * len(outs), **kw
    )(*args)


def selection(source_ref):
    d = source_ref.shape[1]
    rows = lax.broadcasted_iota(jnp.int32, (d, d), 0)
    return (rows == source_ref[...]).astype(bf16)


def change(own_col_ref, group_ref):
    return (own_col_ref[...] == group_ref[...]).astype(bf16)


def moved(f, v, select):
    high = v.astype(bf16)
    return f(high, select) + f((v - high.astype(f32)).astype(bf16), select)


def split_nn(v, parts, cols):
    half = parts[0].shape[0]
    return nn(v[:, :half], parts[0][:, cols]) + nn(v[:, half:], parts[1][:, cols])


def split_nt(v, parts, cols):
    return jnp.concatenate([nt(v, p[:, cols]) for p in parts], axis=1)


def allowed_of(seq_row_ref, seq_col_ref):
    row, col = seq_row_ref[...], seq_col_ref[...]
    t = row.shape[1]
    i = lax.broadcasted_iota(jnp.int32, (t, t), 0)
    j = lax.broadcasted_iota(jnp.int32, (t, t), 1)
    return ((col == row) & (col >= 0) & (j <= i)) | (i == j)


def swap_halves(v):
    lane = lax.broadcasted_iota(jnp.int32, v.shape, 1)
    first = (lane % HD) < (HD // 2)
    return jnp.where(first, pltpu.roll(v, 2 * HD - HD // 2, 1), pltpu.roll(v, HD // 2, 1))


def prep_kernel(tokens, cot, own, group, seq_col, xp, gb, gbg):
    select = selection(own)
    xp[...] = nn(tokens[...], select).astype(bf16)
    live = seq_col[...] >= 0
    gb[...] = jnp.where(live, nn(cot[...], select), 0.0).astype(bf16)
    gbg[...] = jnp.where(live, nn(cot[...], selection(group)), 0.0).astype(bf16)


def attn_kernel(xp, qk0, qk1, vo0, vo1, cos, sin, seq_row, seq_col, n1t, qr, kr, vb, ob, gains, n1):
    d = xp.shape[1]
    qk, vo = (qk0, qk1), (vo0, vo1)
    gt = jnp.concatenate([p[:, 2 * d :] for p in qk], axis=0).astype(f32).T
    gains[...] = gt[0:8]
    x = xp[...].astype(f32)
    r1 = lax.rsqrt(jnp.mean(x * x, axis=-1, keepdims=True) + EPS)
    normed = x * r1 * gt[0:1]
    n1[...] = normed.astype(bf16)
    n1t[...] = normed.T.astype(bf16)
    allowed = allowed_of(seq_row, seq_col)
    pair = 2 * HD
    low = lax.broadcasted_iota(jnp.int32, (x.shape[0], pair), 1) < HD
    scale = HD ** -0.5
    for b in range(d // 256):
        cols = slice(b * 256, (b + 1) * 256)
        q2 = split_nn(n1, qk, cols)
        k2 = split_nn(n1, qk, slice(d + b * 256, d + (b + 1) * 256))
        vb[:, cols] = split_nn(n1, vo, cols).astype(bf16)
        for h in range(2):
            here = slice(h * pair, (h + 1) * pair)
            there = slice(b * 256 + h * pair, b * 256 + (h + 1) * pair)
            q, k = q2[:, here], k2[:, here]
            qr[:, there] = (q * cos[...] + swap_halves(q) * sin[...]).astype(bf16)
            kr[:, there] = (k * cos[...] + swap_halves(k) * sin[...]).astype(bf16)
    for b in range(d // pair):
        cols = slice(b * pair, (b + 1) * pair)
        q, k, v = qr[:, cols], kr[:, cols], vb[:, cols]
        outs = []
        for mine in (low, ~low):
            s = nt(jnp.where(mine, q, jnp.zeros_like(q)), k)
            logits = jnp.where(allowed, s * scale, MASKED)
            e = jnp.exp(logits - jnp.max(logits, axis=-1, keepdims=True))
            p = e / jnp.sum(e, axis=-1, keepdims=True)
            outs.append(nn(p.astype(bf16), v))
        ob[:, cols] = jnp.where(low, outs[0], outs[1]).astype(bf16)


def mid_kernel(xp, ob, vo0, vo1, gains, own_col, group, hmid, n2g):
    d = xp.shape[1]
    h = xp[...].astype(f32) + split_nt(ob[...], (vo0, vo1), slice(d, 2 * d))
    hmid[...] = h
    r2 = lax.rsqrt(jnp.mean(h * h, axis=-1, keepdims=True) + EPS)
    n2g[...] = nn((h * r2 * gains[1:2]).astype(bf16), change(own_col, group)).astype(bf16)


def ff_kernel(n2, gb, *refs):
    ws, (act, both, keep, send, acc) = refs[:PARTS], refs[PARTS:]
    half = n2.shape[0] // 2
    for c, w in enumerate(ws):
        fc = w.shape[1] // 3
        gate = nn(n2[...], w[:, :fc])
        up = nn(n2[...], w[:, fc : 2 * fc])
        dact = nn(gb[...], w[:, 2 * fc :])
        sig = jax.nn.sigmoid(gate)
        silu = gate * sig
        act[:, c * fc : (c + 1) * fc] = (silu * up).astype(bf16)
        at = 2 * c * fc
        both[:, at : at + fc] = (dact * up * sig * (1.0 + gate * (1.0 - sig))).astype(bf16)
        both[:, at + fc : at + 2 * fc] = (dact * silu).astype(bf16)
        part = nt(both[:, at : at + 2 * fc], w[:, : 2 * fc])
        acc[...] = part if c == 0 else acc[...] + part
    keep[...] = acc[:half].astype(bf16)
    send[...] = acc[half:].astype(bf16)


def ff_grad_kernel(n2, gb, act, both, *refs):
    n2t, gbt = refs[-2:]
    n2t[...] = n2[...].astype(f32).T.astype(bf16)
    gbt[...] = gb[...].astype(f32).T.astype(bf16)
    for c in range(PARTS):
        keep, send = refs[2 * c : 2 * c + 2]
        fc = keep.shape[1] // 3
        runs = 2 ** c
        run = n2t.shape[0] // (2 * runs)
        for left, right, cols in (
            (n2t, both[:, 2 * c * fc : 2 * (c + 1) * fc], slice(0, 2 * fc)),
            (gbt, act[:, c * fc : (c + 1) * fc], slice(2 * fc, 3 * fc)),
        ):
            dw = nn(left[...], right).astype(bf16)
            for r in range(runs):
                keep[r * run : (r + 1) * run, cols] = dw[2 * r * run : (2 * r + 1) * run]
                send[r * run : (r + 1) * run, cols] = dw[(2 * r + 1) * run : (2 * r + 2) * run]


def ff_out_kernel(act, *refs):
    ws, (keep, send) = refs[:PARTS], refs[PARTS:]
    half = act.shape[0] // 2
    fc = ws[0].shape[1] // 3
    for ref, rows in ((keep, slice(0, half)), (send, slice(half, 2 * half))):
        ref[...] = sum(nt(act[rows, c * fc : (c + 1) * fc], w[:, 2 * fc :]) for c, w in enumerate(ws)).astype(bf16)


def back_kernel(k1, g1, g2, hmid, gb, gains, vo0, vo1, ob, own_col, group, dh, dob, keep, send, dgain):
    t, d = hmid.shape
    half = d // 2
    total = k1[:t].astype(f32) + g1[:t].astype(f32) + g2[...].astype(f32)
    dn2 = moved(nt, total, change(own_col, group))
    h = hmid[...]
    r2 = lax.rsqrt(jnp.mean(h * h, axis=-1, keepdims=True) + EPS)
    dgain[...] = jnp.broadcast_to(jnp.sum(dn2 * h * r2, axis=0, keepdims=True), dgain.shape)
    dn2 = dn2 * gains[1:2]
    out = gb[...].astype(f32) + r2 * dn2 - h * (r2 * r2 * r2) * jnp.mean(dn2 * h, axis=-1, keepdims=True)
    dh[...] = out
    dob[...] = split_nn(out.astype(bf16), (vo0, vo1), slice(d, 2 * d)).astype(bf16)
    dw = nn(out.T.astype(bf16), ob[...]).astype(bf16)
    keep[...] = dw[:half]
    send[...] = dw[half:]


def attn_back_kernel(qr, kr, vb, dob, n1t, cos, sin, seq_row, seq_col, dq, dk, dv, keep, send):
    t, d = qr.shape
    half = d // 2
    pair = 2 * HD
    allowed = allowed_of(seq_row, seq_col)
    low = lax.broadcasted_iota(jnp.int32, (t, pair), 1) < HD
    scale = HD ** -0.5
    for b in range(d // pair):
        cols = slice(b * pair, (b + 1) * pair)
        q, k, v, do = qr[:, cols], kr[:, cols], vb[:, cols], dob[:, cols]
        dqs, dks, dvs = [], [], []
        for mine in (low, ~low):
            s = nt(jnp.where(mine, q, jnp.zeros_like(q)), k)
            logits = jnp.where(allowed, s * scale, MASKED)
            e = jnp.exp(logits - jnp.max(logits, axis=-1, keepdims=True))
            p = e / jnp.sum(e, axis=-1, keepdims=True)
            dp = nt(jnp.where(mine, do, jnp.zeros_like(do)), v)
            dlogit = p * (dp - jnp.sum(dp * p, axis=-1, keepdims=True))
            ds = jnp.where(allowed, dlogit * scale, 0.0)
            dvs.append(nn(p.T.astype(bf16), do))
            dqs.append(nn(ds.astype(bf16), k))
            dks.append(nn(ds.T.astype(bf16), q))
        dv[:, cols] = jnp.where(low, dvs[0], dvs[1]).astype(bf16)
        for grads, ref in ((dqs, dq), (dks, dk)):
            g = jnp.where(low, grads[0], grads[1])
            ref[:, cols] = (g * cos[...] - swap_halves(g) * sin[...]).astype(bf16)
    for part, ref in enumerate((dv, dq)):
        for b in range(d // 256):
            dw = nn(n1t[...], ref[:, b * 256 : (b + 1) * 256]).astype(bf16)
            cols = slice(part * d + b * 256, part * d + (b + 1) * 256)
            keep[:, cols] = dw[:half]
            send[:, cols] = dw[half:]


def last_kernel(dq, dk, dv, qk0, qk1, vo0, vo1, n1t, xp, dh, gains, dgain2, own, dtok, keep, send):
    _, d = xp.shape
    half = d // 2
    qk, vo = (qk0, qk1), (vo0, vo1)
    dn1 = (split_nt(dq[...], qk, slice(0, d)) + split_nt(dk[...], qk, slice(d, 2 * d))
           + split_nt(dv[...], vo, slice(0, d)))
    dw = nn(n1t[...], dk[...]).astype(bf16)
    keep[:, :d] = dw[:half]
    send[:, :d] = dw[half:]
    x = xp[...].astype(f32)
    r1 = lax.rsqrt(jnp.mean(x * x, axis=-1, keepdims=True) + EPS)
    dgain1 = jnp.sum(dn1 * x * r1, axis=0, keepdims=True)
    row = lax.broadcasted_iota(jnp.int32, (128, d), 0)
    both = jnp.where(row == 0, dgain1, jnp.where(row == 1, dgain2[0:1], 0.0)).T.astype(bf16)
    keep[:, d:] = both[:half]
    send[:, d:] = both[half:]
    g = dn1 * gains[0:1]
    out = dh[...] + r1 * g - x * (r1 * r1 * r1) * jnp.mean(g * x, axis=-1, keepdims=True)
    dtok[...] = nt(out.astype(bf16), selection(own)).astype(bf16)


def out_kernel(k1, g1, g2, hmid, own, group, out):
    t = hmid.shape[0]
    total = k1[:t].astype(f32) + g1[:t].astype(f32) + g2[...].astype(f32)
    out[...] = (moved(nt, total, selection(group)) + moved(nt, hmid[...], selection(own))).astype(bf16)


def make_on_device(n):
    first, second = gather_orders(n)
    axis_bits = tuple(reversed(first))
    axis_of = {b: i for i, b in enumerate(axis_bits)}
    k = len(axis_bits)
    assert axis_bits[0] == first[-1] == second[-1]
    high = [b for b in first if b not in LOW]
    ff_orders = (tuple(high), tuple(high[:-2]) + (high[-1], high[-2]))
    ff_bits = tuple(reversed(high)) + tuple(reversed(LOW))
    ff_axis = {b: i for i, b in enumerate(ff_bits)}

    def swap(a, b):
        return lax.ppermute(a, "dp", [(i, i ^ b) for i in range(n)])

    def gather(shard, order):
        a = shard.reshape((1,) * k + shard.shape)
        for i, b in enumerate(order):
            got = swap(a, b)
            if i == k - 1:
                return tuple(v.reshape((n * shard.shape[0] // 2,) + shard.shape[1:]) for v in (a, got))
            a = jnp.concatenate([a, got], axis=axis_of[b])

    def reduce(keep, send, steps, axis, last):
        for i, b in enumerate(steps):
            got = swap(send, b)
            if i == len(steps) - 1:
                return (keep.astype(f32) + got.astype(f32)).astype(last)
            ax = axis[steps[i + 1]]
            part = lambda v, at: lax.slice_in_dim(v, at, at + 1, axis=ax).astype(f32)
            send, keep = (
                (part(keep, 1) + part(got, 1)).astype(bf16),
                (part(keep, 0) + part(got, 0)).astype(bf16),
            )

    def scatter(keep, send, order):
        rows, cols = keep.shape[0] * 2 // n, keep.shape[1]
        shape = (1,) + (2,) * (k - 1) + (rows, cols)
        a = reduce(keep.reshape(shape), send.reshape(shape), tuple(reversed(order)), axis_of, f32)
        return a.reshape(rows, cols)

    def on_device(tokens, seq_ids, positions, cotangent, attn_gain, w_query, w_key, w_value, w_output,
                  mlp_gain, w_gate, w_up, w_down):
        toks, d = tokens.shape
        rows = d // n
        ff = w_gate.shape[1]
        share = 2 ** len(LOW)
        fc = ff // share // PARTS
        half = d // 2
        me = lax.axis_index("dp")

        def source_of(bits, base):
            slot = jnp.arange(d, dtype=jnp.int32) // rows
            owner = jnp.zeros_like(slot)
            for i, b in enumerate(bits):
                owner = owner + ((slot >> (k - 1 - i)) & 1) * b
            return (owner ^ base) * rows + jnp.arange(d, dtype=jnp.int32) % rows

        own_line = source_of(axis_bits, me)
        own, own_col = own_line[None, :], own_line[:, None]
        group = source_of(ff_bits, me - me % share)[None, :]
        odd = {b: (me & b) != 0 for b in LOW}

        def pick(b, x, y):
            return jnp.where(odd[b], y, x), jnp.where(odd[b], x, y)

        gains = jnp.pad(jnp.stack([attn_gain, mlp_gain], axis=1), ((0, 0), (0, 126)))
        qk = gather(jnp.concatenate([w_query, w_key, gains], axis=1), first)
        vo = gather(jnp.concatenate([w_value, w_output.T], axis=1), second)
        a = jnp.stack([v.reshape(rows, share, PARTS, fc) for v in (w_gate, w_up, w_down.T)], axis=3)
        a = a.reshape((1,) * k + (rows, 2, 2, PARTS * 3 * fc))
        for i, b in enumerate(LOW):
            keep, send = pick(b, a[..., 0, :] if i else a[..., 0, :, :], a[..., 1, :] if i else a[..., 1, :, :])
            got = swap(send, b)
            a = jnp.concatenate(pick(b, keep, got), axis=ff_axis[b])
        wff = []
        for c in range(PARTS):
            w = a[..., c * 3 * fc : (c + 1) * 3 * fc]
            for b in ff_orders[c]:
                w = jnp.concatenate([w, swap(w, b)], axis=ff_axis[b])
            wff.append(w.reshape(d, 3 * fc))
        freq = jnp.exp(jnp.arange(HD // 2, dtype=f32) * (-2.0 * math.log(THETA) / HD))
        angles = positions.astype(f32)[:, None] * freq[None, :]
        cosine, sine = jnp.cos(angles), jnp.sin(angles)
        cos2 = jnp.concatenate([cosine] * 4, axis=1)
        sin2 = jnp.concatenate([-sine, sine, -sine, sine], axis=1)
        seq_row, seq_col = seq_ids[None, :], seq_ids[:, None]
        act, mat, wide = ((toks, d), bf16), ((d, toks), bf16), ((toks, d), f32)

        def group_gather(v):
            for b in LOW:
                v = jnp.concatenate([v, swap(v, b)], axis=0)
            return v

        def group_halve(keep, send):
            g1 = swap(send, LOW[1])
            g2 = swap((keep[toks:].astype(f32) + g1[toks:].astype(f32)).astype(bf16), LOW[0])
            return keep, g1, g2

        xp, gb, gbg = call(prep_kernel, [act, act, act], tokens, cotangent, own, group, seq_col)
        gb4 = group_gather(gbg)
        n1t, qr, kr, vb, ob, gains, _ = call(
            attn_kernel, [mat, act, act, act, act, ((8, d), f32), act],
            xp, *qk, *vo, cos2, sin2, seq_row, seq_col)
        hmid, n2g = call(mid_kernel, [wide, act], xp, ob, *vo, gains, own_col, group)
        n24 = group_gather(n2g)
        tg = share * toks
        hidden = PARTS * fc
        pairs = [((tg // 2, d), bf16)] * 2
        acts, both, keep, send = call(
            ff_kernel, [((tg, hidden), bf16), ((tg, 2 * hidden), bf16)] + pairs, n24, gb4, *wff,
            scratch_shapes=[pltpu.VMEM((tg, d), f32)])
        dn2 = group_halve(keep, send)
        grads = call(
            ff_grad_kernel, [((half, 3 * fc), bf16)] * (2 * PARTS), n24, gb4, acts, both,
            scratch_shapes=[pltpu.VMEM((d, tg), bf16)] * 2)
        y = group_halve(*call(ff_out_kernel, pairs, acts, *wff))
        parts = []
        for c in range(PARTS):
            steps = tuple(reversed(ff_orders[c]))
            shape = tuple(1 if b == steps[0] else 2 for b in ff_bits) + (rows, 3 * fc)
            parts.append(reduce(*(v.reshape(shape) for v in grads[2 * c : 2 * c + 2]), steps, ff_axis, bf16))
        a = jnp.stack(parts, axis=-2)
        for b in reversed(LOW):
            ax = ff_axis[b]
            keep, send = pick(b, *(lax.slice_in_dim(a, at, at + 1, axis=ax) for at in (0, 1)))
            a = jnp.stack(pick(b, keep, swap(send, b)), axis=k + 1)
        a = a.reshape(rows, share, PARTS, 3, fc).astype(f32)
        d_gate, d_up, d_down = (a[:, :, :, i].reshape(rows, ff) for i in range(3))
        dh, dob, keep, send, dgain2 = call(
            back_kernel, [wide, act, ((half, d), bf16), ((half, d), bf16), ((8, d), f32)],
            *dn2, hmid, gb, gains, *vo, ob, own_col, group)
        d_wo = scatter(keep, send, first)
        dq, dk, dv, keep, send = call(
            attn_back_kernel, [act, act, act, ((half, 2 * d), bf16), ((half, 2 * d), bf16)],
            qr, kr, vb, dob, n1t, cos2, sin2, seq_row, seq_col)
        d_vq = scatter(keep, send, second)
        dtok, keep, send = call(
            last_kernel, [act, ((half, d + 128), bf16), ((half, d + 128), bf16)],
            dq, dk, dv, *qk, *vo, n1t, xp, dh, gains, dgain2, own)
        d_kg = scatter(keep, send, first)
        (out,) = call(out_kernel, [act], *y, hmid, own, group)
        return (out, dtok, d_kg[:, d], d_vq[:, d:], d_kg[:, :d], d_vq[:, :d], d_wo.T, d_kg[:, d + 1],
                d_gate, d_up, d_down.T)

    return on_device


def solution(mesh):
    rows, cols, vec = P("dp", None), P(None, "dp"), P("dp")
    in_specs = (rows, vec, vec, rows, vec, rows, rows, rows, cols, vec, rows, rows, cols)
    out_specs = (rows, rows, vec, rows, rows, rows, cols, vec, rows, rows, cols)
    return jax.shard_map(make_on_device(mesh.shape["dp"]), mesh=mesh, in_specs=in_specs, out_specs=out_specs, check_vma=False)
```

```python
import math

import jax
import jax.numpy as jnp
import numpy as np
from jax import lax
from jax.experimental import pallas as pl
from jax.experimental.pallas import tpu as pltpu
from jax.sharding import PartitionSpec as P


HD = 64
LOW = (2, 1)
PARTS = 2
VMEM = 20 * 2**20
EPS = 1e-05
MASKED = -1e30
THETA = 10000.0


f32 = jnp.float32
bf16 = jnp.bfloat16


def gather_orders(n):
    if n == 32:
        return (16, 8, 2, 4, 1), (16, 8, 4, 2, 1)
    bits = [1 << k for k in range(n.bit_length() - 1)]
    order = tuple(reversed(bits))
    return order, order


def nn(a, b):
    return jnp.dot(a, b, preferred_element_type=f32)


def nt(a, b):
    return lax.dot_general(a, b, (((1,), (1,)), ((), ())), preferred_element_type=f32)


def call(kernel, outs, *args, grant=VMEM, **kw):
    out_shape = [jax.ShapeDtypeStruct(s, d) for s, d in outs]
    vmem = pl.BlockSpec(memory_space=pltpu.VMEM)
    smem = pl.BlockSpec(memory_space=pltpu.SMEM)
    return pl.pallas_call(
        kernel,
        out_shape=out_shape,
        in_specs=[smem if v.size == 1 else vmem for v in args],
        out_specs=[vmem] * len(outs),
        compiler_params=pltpu.CompilerParams(vmem_limit_bytes=grant),
        **kw,
    )(*args)


def moved(f, v, select):
    high = v.astype(bf16)
    return f(high, select) + f((v - high.astype(f32)).astype(bf16), select)


def split_nn(v, parts, cols):
    half = parts[0].shape[0]
    return nn(v[:, :half], parts[0][:, cols]) + nn(v[:, half:], parts[1][:, cols])


def split_nt(v, parts, cols):
    return jnp.concatenate([nt(v, p[:, cols]) for p in parts], axis=1)


def allowed_of(seq_row_ref, seq_col_ref):
    row, col = seq_row_ref[...], seq_col_ref[...]
    t = row.shape[1]
    i = lax.broadcasted_iota(jnp.int32, (t, t), 0)
    j = lax.broadcasted_iota(jnp.int32, (t, t), 1)
    return ((col == row) & (col >= 0) & (j <= i)) | (i == j)


def swap_halves(v):
    lane = lax.broadcasted_iota(jnp.int32, v.shape, 1)
    first = (lane % HD) < (HD // 2)
    return jnp.where(first, pltpu.roll(v, 2 * HD - HD // 2, 1), pltpu.roll(v, HD // 2, 1))


def pack_kernel(me, attn_gain, mlp_gain, wq, wk, wv, wo, wgate, wup, wdown, qk, vo, keep, send):
    rows, d = wq.shape
    qk[:, :d] = wq[...]
    qk[:, d : 2 * d] = wk[...]
    spot = lax.broadcasted_iota(jnp.int32, (rows, rows), 0) == lax.broadcasted_iota(jnp.int32, (rows, rows), 1)
    column = lambda ref: jnp.sum(jnp.where(spot, ref[...].astype(f32), 0.0), axis=1, keepdims=True)
    lane = lax.broadcasted_iota(jnp.int32, (rows, 128), 1)
    both = jnp.where(lane == 0, column(attn_gain), jnp.where(lane == 1, column(mlp_gain), 0.0))
    qk[:, 2 * d :] = both.astype(bf16)
    vo[:, :d] = wv[...]
    vo[:, d:] = wo[...]
    low = me[0] % (2 * LOW[0])
    hidden = wgate.shape[1] // 4
    fc = hidden // PARTS
    for ref, flip in ((keep, 0), (send, LOW[0])):
        for i, other in enumerate((0, LOW[1])):
            base = (low ^ (flip + other)) * hidden
            for c in range(PARTS):
                for m, w in enumerate((wgate, wup, wdown)):
                    at = i * 3 * hidden + (c * 3 + m) * fc
                    ref[:, at : at + fc] = w[:, pl.ds(pl.multiple_of(base + c * fc, 128), fc)]


def unpack_kernel(me, *refs):
    parts, outs = refs[:4], refs[4:]
    low = me[0] % (2 * LOW[0])
    hidden = outs[0].shape[1] // 4
    fc = hidden // PARTS
    for ref, flip in zip(parts, (0, LOW[1], LOW[0], LOW[0] + LOW[1])):
        base = (low ^ flip) * hidden
        for c in range(PARTS):
            for m, out in enumerate(outs):
                at = (c * 3 + m) * fc
                out[:, pl.ds(pl.multiple_of(base + c * fc, 128), fc)] = ref[:, at : at + fc].astype(f32)


def prep_kernel(me, tokens, cot, places, live, xp, gb, gbg, own_sel, group_sel, change):
    d = tokens.shape[1]
    rows = places[4, 0]
    share = 2 * LOW[0]
    own = (places[0:1] ^ me[0]) * rows + places[1:2]
    group = (places[2:3] ^ (me[0] - me[0] % share)) * rows + places[3:4]
    source = lax.broadcasted_iota(jnp.int32, (d, d), 0)
    own_sel[...] = (source == own).astype(bf16)
    group_sel[...] = (source == group).astype(bf16)
    own_col = jnp.broadcast_to(own.astype(f32), (128, d)).T[:, 0:1]
    change[...] = (own_col == group.astype(f32)).astype(bf16)
    xp[...] = nn(tokens[...], own_sel[...]).astype(bf16)
    gb[...] = (nn(cot[...], own_sel[...]) * live[...]).astype(bf16)
    gbg[...] = (nn(cot[...], group_sel[...]) * live[...]).astype(bf16)


def attn_kernel(xp, qk0, qk1, vo0, vo1, cos, sin, seq_row, seq_col, n1t, qr, kr, vb, ob, gains, n1):
    d = xp.shape[1]
    qk, vo = (qk0, qk1), (vo0, vo1)
    gt = jnp.concatenate([p[:, 2 * d :] for p in qk], axis=0).astype(f32).T
    gains[...] = gt[0:8]
    x = xp[...].astype(f32)
    r1 = lax.rsqrt(jnp.mean(x * x, axis=-1, keepdims=True) + EPS)
    normed = x * r1 * gt[0:1]
    n1[...] = normed.astype(bf16)
    n1t[...] = normed.T.astype(bf16)
    allowed = allowed_of(seq_row, seq_col)
    pair = 2 * HD
    low = lax.broadcasted_iota(jnp.int32, (x.shape[0], pair), 1) < HD
    scale = HD ** -0.5
    for b in range(d // 256):
        cols = slice(b * 256, (b + 1) * 256)
        q2 = split_nn(n1, qk, cols)
        k2 = split_nn(n1, qk, slice(d + b * 256, d + (b + 1) * 256))
        vb[:, cols] = split_nn(n1, vo, cols).astype(bf16)
        for h in range(2):
            here = slice(h * pair, (h + 1) * pair)
            there = slice(b * 256 + h * pair, b * 256 + (h + 1) * pair)
            q, k = q2[:, here], k2[:, here]
            qr[:, there] = (q * cos[...] + swap_halves(q) * sin[...]).astype(bf16)
            kr[:, there] = (k * cos[...] + swap_halves(k) * sin[...]).astype(bf16)
    for b in range(d // pair):
        cols = slice(b * pair, (b + 1) * pair)
        q, k, v = qr[:, cols], kr[:, cols], vb[:, cols]
        outs = []
        for mine in (low, ~low):
            s = nt(jnp.where(mine, q, jnp.zeros_like(q)), k)
            logits = jnp.where(allowed, s * scale, MASKED)
            e = jnp.exp(logits - jnp.max(logits, axis=-1, keepdims=True))
            p = e / jnp.sum(e, axis=-1, keepdims=True)
            outs.append(nn(p.astype(bf16), v))
        ob[:, cols] = jnp.where(low, outs[0], outs[1]).astype(bf16)


def mid_kernel(xp, ob, vo0, vo1, gains, change, hmid, n2g):
    d = xp.shape[1]
    h = xp[...].astype(f32) + split_nt(ob[...], (vo0, vo1), slice(d, 2 * d))
    hmid[...] = h
    r2 = lax.rsqrt(jnp.mean(h * h, axis=-1, keepdims=True) + EPS)
    n2g[...] = nn((h * r2 * gains[1:2]).astype(bf16), change[...]).astype(bf16)


def ff_kernel(n2, gb, *refs):
    ws, (act, both, keep, send, acc) = refs[:PARTS], refs[PARTS:]
    half = n2.shape[0] // 2
    for c, w in enumerate(ws):
        fc = w.shape[1] // 3
        gate = nn(n2[...], w[:, :fc])
        up = nn(n2[...], w[:, fc : 2 * fc])
        dact = nn(gb[...], w[:, 2 * fc :])
        sig = jax.nn.sigmoid(gate)
        silu = gate * sig
        act[:, c * fc : (c + 1) * fc] = (silu * up).astype(bf16)
        at = 2 * c * fc
        both[:, at : at + fc] = (dact * up * sig * (1.0 + gate * (1.0 - sig))).astype(bf16)
        both[:, at + fc : at + 2 * fc] = (dact * silu).astype(bf16)
        part = nt(both[:, at : at + 2 * fc], w[:, : 2 * fc])
        acc[...] = part if c == 0 else acc[...] + part
    keep[...] = acc[:half].astype(bf16)
    send[...] = acc[half:].astype(bf16)


def ff_grad_kernel(n2, gb, act, both, *refs):
    n2t, gbt = refs[-2:]
    n2t[...] = n2[...].astype(f32).T.astype(bf16)
    gbt[...] = gb[...].astype(f32).T.astype(bf16)
    for c in range(PARTS):
        keep, send = refs[2 * c : 2 * c + 2]
        fc = keep.shape[1] // 3
        runs = 2 ** c
        run = n2t.shape[0] // (2 * runs)
        for left, right, cols in (
            (n2t, both[:, 2 * c * fc : 2 * (c + 1) * fc], slice(0, 2 * fc)),
            (gbt, act[:, c * fc : (c + 1) * fc], slice(2 * fc, 3 * fc)),
        ):
            dw = nn(left[...], right).astype(bf16)
            for r in range(runs):
                keep[r * run : (r + 1) * run, cols] = dw[2 * r * run : (2 * r + 1) * run]
                send[r * run : (r + 1) * run, cols] = dw[(2 * r + 1) * run : (2 * r + 2) * run]


def ff_out_kernel(act, *refs):
    ws, (keep, send) = refs[:PARTS], refs[PARTS:]
    half = act.shape[0] // 2
    fc = ws[0].shape[1] // 3
    for ref, rows in ((keep, slice(0, half)), (send, slice(half, 2 * half))):
        ref[...] = sum(nt(act[rows, c * fc : (c + 1) * fc], w[:, 2 * fc :]) for c, w in enumerate(ws)).astype(bf16)


def back_kernel(k1, g1, g2, hmid, gb, gains, vo0, vo1, ob, change, dh, dob, keep, send, dgain):
    t, d = hmid.shape
    half = d // 2
    total = k1[:t].astype(f32) + g1[:t].astype(f32) + g2[...].astype(f32)
    dn2 = moved(nt, total, change[...])
    h = hmid[...]
    r2 = lax.rsqrt(jnp.mean(h * h, axis=-1, keepdims=True) + EPS)
    dgain[...] = jnp.broadcast_to(jnp.sum(dn2 * h * r2, axis=0, keepdims=True), dgain.shape)
    dn2 = dn2 * gains[1:2]
    out = gb[...].astype(f32) + r2 * dn2 - h * (r2 * r2 * r2) * jnp.mean(dn2 * h, axis=-1, keepdims=True)
    dh[...] = out
    dob[...] = split_nn(out.astype(bf16), (vo0, vo1), slice(d, 2 * d)).astype(bf16)
    dw = nn(out.T.astype(bf16), ob[...]).astype(bf16)
    keep[...] = dw[:half]
    send[...] = dw[half:]


def attn_back_kernel(qr, kr, vb, dob, n1t, cos, sin, seq_row, seq_col, dq, dk, dv, keep, send):
    t, d = qr.shape
    half = d // 2
    pair = 2 * HD
    allowed = allowed_of(seq_row, seq_col)
    low = lax.broadcasted_iota(jnp.int32, (t, pair), 1) < HD
    scale = HD ** -0.5
    for b in range(d // pair):
        cols = slice(b * pair, (b + 1) * pair)
        q, k, v, do = qr[:, cols], kr[:, cols], vb[:, cols], dob[:, cols]
        dqs, dks, dvs = [], [], []
        for mine in (low, ~low):
            s = nt(jnp.where(mine, q, jnp.zeros_like(q)), k)
            logits = jnp.where(allowed, s * scale, MASKED)
            e = jnp.exp(logits - jnp.max(logits, axis=-1, keepdims=True))
            p = e / jnp.sum(e, axis=-1, keepdims=True)
            dp = nt(jnp.where(mine, do, jnp.zeros_like(do)), v)
            dlogit = p * (dp - jnp.sum(dp * p, axis=-1, keepdims=True))
            ds = jnp.where(allowed, dlogit * scale, 0.0)
            dvs.append(nn(p.T.astype(bf16), do))
            dqs.append(nn(ds.astype(bf16), k))
            dks.append(nn(ds.T.astype(bf16), q))
        dv[:, cols] = jnp.where(low, dvs[0], dvs[1]).astype(bf16)
        for grads, ref in ((dqs, dq), (dks, dk)):
            g = jnp.where(low, grads[0], grads[1])
            ref[:, cols] = (g * cos[...] - swap_halves(g) * sin[...]).astype(bf16)
    for part, ref in enumerate((dv, dq)):
        for b in range(d // 256):
            dw = nn(n1t[...], ref[:, b * 256 : (b + 1) * 256]).astype(bf16)
            cols = slice(part * d + b * 256, part * d + (b + 1) * 256)
            keep[:, cols] = dw[:half]
            send[:, cols] = dw[half:]


def last_kernel(dq, dk, dv, qk0, qk1, vo0, vo1, n1t, xp, dh, gains, dgain2, own_sel, dtok, keep, send):
    _, d = xp.shape
    half = d // 2
    qk, vo = (qk0, qk1), (vo0, vo1)
    dn1 = (split_nt(dq[...], qk, slice(0, d)) + split_nt(dk[...], qk, slice(d, 2 * d))
           + split_nt(dv[...], vo, slice(0, d)))
    dw = nn(n1t[...], dk[...]).astype(bf16)
    keep[:, :d] = dw[:half]
    send[:, :d] = dw[half:]
    x = xp[...].astype(f32)
    r1 = lax.rsqrt(jnp.mean(x * x, axis=-1, keepdims=True) + EPS)
    dgain1 = jnp.sum(dn1 * x * r1, axis=0, keepdims=True)
    row = lax.broadcasted_iota(jnp.int32, (128, d), 0)
    both = jnp.where(row == 0, dgain1, jnp.where(row == 1, dgain2[0:1], 0.0)).T.astype(bf16)
    keep[:, d:] = both[:half]
    send[:, d:] = both[half:]
    g = dn1 * gains[0:1]
    out = dh[...] + r1 * g - x * (r1 * r1 * r1) * jnp.mean(g * x, axis=-1, keepdims=True)
    dtok[...] = nt(out.astype(bf16), own_sel[...]).astype(bf16)


def out_kernel(k1, g1, g2, hmid, own_sel, group_sel, out):
    t = hmid.shape[0]
    total = k1[:t].astype(f32) + g1[:t].astype(f32) + g2[...].astype(f32)
    out[...] = (moved(nt, total, group_sel[...]) + moved(nt, hmid[...], own_sel[...])).astype(bf16)


def make_on_device(n):
    first, second = gather_orders(n)
    axis_bits = tuple(reversed(first))
    axis_of = {b: i for i, b in enumerate(axis_bits)}
    k = len(axis_bits)
    assert axis_bits[0] == first[-1] == second[-1]
    high = sorted((b for b in first if b not in LOW), reverse=True)
    ff_orders = (tuple(high), (high[-1],) + tuple(high[:-1]))
    ff_bits = tuple(reversed(high)) + tuple(reversed(LOW))
    ff_axis = {b: i for i, b in enumerate(ff_bits)}

    def swap(a, b):
        return lax.ppermute(a, "dp", [(i, i ^ b) for i in range(n)])

    def gather(shard, order):
        a = shard.reshape((1,) * k + shard.shape)
        for i, b in enumerate(order):
            got = swap(a, b)
            if i == k - 1:
                return tuple(v.reshape((n * shard.shape[0] // 2,) + shard.shape[1:]) for v in (a, got))
            a = jnp.concatenate([a, got], axis=axis_of[b])

    def reduce(keep, send, steps, axis, last):
        for i, b in enumerate(steps):
            got = swap(send, b)
            if i == len(steps) - 1:
                return (keep.astype(f32) + got.astype(f32)).astype(last)
            ax = axis[steps[i + 1]]
            part = lambda v, at: lax.slice_in_dim(v, at, at + 1, axis=ax).astype(f32)
            send, keep = (
                (part(keep, 1) + part(got, 1)).astype(bf16),
                (part(keep, 0) + part(got, 0)).astype(bf16),
            )

    def scatter(keep, send, order):
        rows, cols = keep.shape[0] * 2 // n, keep.shape[1]
        shape = (1,) + (2,) * (k - 1) + (rows, cols)
        a = reduce(keep.reshape(shape), send.reshape(shape), tuple(reversed(order)), axis_of, f32)
        return a.reshape(rows, cols)

    def on_device(tokens, seq_ids, positions, cotangent, attn_gain, w_query, w_key, w_value, w_output,
                  mlp_gain, w_gate, w_up, w_down):
        toks, d = tokens.shape
        rows = d // n
        ff = w_gate.shape[1]
        share = 2 ** len(LOW)
        fc = ff // share // PARTS
        half = d // 2
        me = lax.axis_index("dp")

        def places_of(bits):
            slot = np.arange(d) // rows
            return sum(((slot >> (k - 1 - i)) & 1) * b for i, b in enumerate(bits)), np.arange(d) % rows

        places = jnp.asarray(np.stack([*places_of(axis_bits), *places_of(ff_bits), np.full(d, rows)]), jnp.int32)
        me1 = me[None]
        odd = {b: (me & b) != 0 for b in LOW}

        def pick(b, x, y):
            return jnp.where(odd[b], y, x), jnp.where(odd[b], x, y)

        shards = [((rows, 2 * d + 128), bf16), ((rows, 2 * d), bf16)] + [((rows, 2 * ff * 3 // share), bf16)] * 2
        part_qk, part_vo, keep, send = call(
            pack_kernel, shards, me1, attn_gain[None, :], mlp_gain[None, :], w_query, w_key, w_value, w_output.T,
            w_gate, w_up, w_down.T, grant=3 * VMEM)
        lead = lambda v: v.reshape((1,) * k + v.shape)
        a = jnp.concatenate(pick(LOW[0], lead(keep), lead(swap(send, LOW[0]))), axis=ff_axis[LOW[0]])
        mine = ff * 3 // share
        got = swap(a[..., mine:], LOW[1])
        a = jnp.concatenate(pick(LOW[1], a[..., :mine], got), axis=ff_axis[LOW[1]])
        qk = gather(part_qk, first)
        vo = gather(part_vo, second)
        wff = []
        for c in range(PARTS):
            w = a[..., c * 3 * fc : (c + 1) * 3 * fc]
            for b in ff_orders[c]:
                got = swap(w, b)
                w = jnp.concatenate([w, got], axis=ff_axis[b])
            wff.append(w.reshape(d, 3 * fc))
        freq = jnp.exp(jnp.arange(HD // 2, dtype=f32) * (-2.0 * math.log(THETA) / HD))
        angles = positions.astype(f32)[:, None] * freq[None, :]
        cosine, sine = jnp.cos(angles), jnp.sin(angles)
        cos2 = jnp.concatenate([cosine] * 4, axis=1)
        sin2 = jnp.concatenate([-sine, sine, -sine, sine], axis=1)
        seq_row, seq_col = seq_ids[None, :], seq_ids[:, None]
        act, mat, wide = ((toks, d), bf16), ((d, toks), bf16), ((toks, d), f32)

        def group_gather(v):
            for b in LOW:
                got = swap(v, b)
                v = jnp.concatenate([v, got], axis=0)
            return v

        def group_halve(keep, send):
            g1 = swap(send, LOW[1])
            v = (keep[toks:].astype(f32) + g1[toks:].astype(f32)).astype(bf16)
            return keep, g1, swap(v, LOW[0])

        live = (seq_col >= 0).astype(f32)
        square = ((d, d), bf16)
        xp, gb, gbg, own_sel, group_sel, change = call(
            prep_kernel, [act, act, act, square, square, square], me1, tokens, cotangent, places, live)
        gb4 = group_gather(gbg)
        n1t, qr, kr, vb, ob, gains, _ = call(
            attn_kernel, [mat, act, act, act, act, ((8, d), f32), act],
            xp, *qk, *vo, cos2, sin2, seq_row, seq_col)
        hmid, n2g = call(mid_kernel, [wide, act], xp, ob, *vo, gains, change)
        n24 = group_gather(n2g)
        tg = share * toks
        hidden = PARTS * fc
        pairs = [((tg // 2, d), bf16)] * 2
        acts, both, keep, send = call(
            ff_kernel, [((tg, hidden), bf16), ((tg, 2 * hidden), bf16)] + pairs, n24, gb4, *wff,
            scratch_shapes=[pltpu.VMEM((tg, d), f32)])
        dn2 = group_halve(keep, send)
        grads = call(
            ff_grad_kernel, [((half, 3 * fc), bf16)] * (2 * PARTS), n24, gb4, acts, both,
            scratch_shapes=[pltpu.VMEM((d, tg), bf16)] * 2)
        y = group_halve(*call(ff_out_kernel, pairs, acts, *wff))
        parts = []
        for c in range(PARTS):
            steps = tuple(reversed(ff_orders[c]))
            shape = tuple(1 if b == steps[0] else 2 for b in ff_bits) + (rows, 3 * fc)
            parts.append(reduce(*(v.reshape(shape) for v in grads[2 * c : 2 * c + 2]), steps, ff_axis, bf16))
        a = jnp.concatenate(parts, axis=-1).reshape(2, 2, rows, mine)
        pair1 = pick(LOW[1], a[0], a[1])
        got1 = swap(pair1[1], LOW[1])
        kept, sent = zip(*(pick(LOW[0], v[0], v[1]) for v in (pair1[0], got1)))
        got2 = swap(jnp.stack(sent), LOW[0])
        d_gate, d_up, d_down = call(
            unpack_kernel, [((rows, ff), f32)] * 3, me1, *kept, got2[0], got2[1])
        dh, dob, keep, send, dgain2 = call(
            back_kernel, [wide, act, ((half, d), bf16), ((half, d), bf16), ((8, d), f32)],
            *dn2, hmid, gb, gains, *vo, ob, change)
        d_wo = scatter(keep, send, second)
        dq, dk, dv, keep, send = call(
            attn_back_kernel, [act, act, act, ((half, 2 * d), bf16), ((half, 2 * d), bf16)],
            qr, kr, vb, dob, n1t, cos2, sin2, seq_row, seq_col)
        d_vq = scatter(keep, send, first)
        dtok, keep, send = call(
            last_kernel, [act, ((half, d + 128), bf16), ((half, d + 128), bf16)],
            dq, dk, dv, *qk, *vo, n1t, xp, dh, gains, dgain2, own_sel)
        d_kg = scatter(keep, send, second)
        (out,) = call(out_kernel, [act], *y, hmid, own_sel, group_sel)
        return (out, dtok, d_kg[:, d], d_vq[:, d:], d_kg[:, :d], d_vq[:, :d], d_wo.T, d_kg[:, d + 1],
                d_gate, d_up, d_down.T)

    return on_device


def solution(mesh):
    rows, cols, vec = P("dp", None), P(None, "dp"), P("dp")
    in_specs = (rows, vec, vec, rows, vec, rows, rows, rows, cols, vec, rows, rows, cols)
    out_specs = (rows, rows, vec, rows, rows, rows, cols, vec, rows, rows, cols)
    n = mesh.shape["dp"]
    return jax.shard_map(make_on_device(n), mesh=mesh, in_specs=in_specs, out_specs=out_specs, check_vma=False)
```

```python
import math

import jax
import jax.numpy as jnp
import numpy as np
from jax import lax
from jax.experimental import pallas as pl
from jax.experimental.pallas import tpu as pltpu
from jax.sharding import PartitionSpec as P


HD = 64
LOW = (2, 1)
PARTS = 2
VMEM = 20 * 2**20
EPS = 1e-05
MASKED = -1e30
THETA = 10000.0


f32 = jnp.float32
bf16 = jnp.bfloat16


def gather_orders(n):
    if n == 32:
        return (16, 8, 2, 4, 1), (16, 8, 4, 2, 1)
    bits = [1 << k for k in range(n.bit_length() - 1)]
    order = tuple(reversed(bits))
    return order, order


def nn(a, b):
    return jnp.dot(a, b, preferred_element_type=f32)


def nt(a, b):
    return lax.dot_general(a, b, (((1,), (1,)), ((), ())), preferred_element_type=f32)


def call(kernel, outs, *args, fetch=True, grant=VMEM, **kw):
    out_shape = [jax.ShapeDtypeStruct(s, d) for s, d in outs]
    vmem = pl.BlockSpec(memory_space=pltpu.VMEM)
    smem = pl.BlockSpec(memory_space=pltpu.SMEM)
    hbm = pl.BlockSpec(memory_space=pltpu.HBM)
    return pl.pallas_call(
        kernel,
        out_shape=out_shape,
        in_specs=[smem if v.size == 1 else vmem if fetch else hbm for v in args],
        out_specs=[vmem] * len(outs),
        compiler_params=pltpu.CompilerParams(vmem_limit_bytes=grant),
        **kw,
    )(*args)


def moved(f, v, select):
    high = v.astype(bf16)
    return f(high, select) + f((v - high.astype(f32)).astype(bf16), select)


def split_nn(v, parts, cols):
    half = parts[0].shape[0]
    return nn(v[:, :half], parts[0][:, cols]) + nn(v[:, half:], parts[1][:, cols])


def split_nt(v, parts, cols):
    return jnp.concatenate([nt(v, p[:, cols]) for p in parts], axis=1)


def column_of(row):
    t = row.shape[1]
    i = lax.broadcasted_iota(jnp.int32, (t, t), 0)
    j = lax.broadcasted_iota(jnp.int32, (t, t), 1)
    return jnp.sum(jnp.where(i == j, row.astype(f32), 0.0), axis=1, keepdims=True)


def allowed_of(seq_ref):
    row = seq_ref[...].astype(f32)
    col = column_of(row)
    t = row.shape[1]
    i = lax.broadcasted_iota(jnp.int32, (t, t), 0)
    j = lax.broadcasted_iota(jnp.int32, (t, t), 1)
    return ((col == row) & (col >= 0.0) & (j <= i)) | (i == j)


def swap_halves(v):
    lane = lax.broadcasted_iota(jnp.int32, v.shape, 1)
    first = (lane % HD) < (HD // 2)
    return jnp.where(first, pltpu.roll(v, 2 * HD - HD // 2, 1), pltpu.roll(v, HD // 2, 1))


def pack_kernel(me, attn_gain, mlp_gain, wq, wk, wv, wo, wgate, wup, wdown, qk, vo, keep, send, gain1, gain2, sems):
    rows, d = wq.shape
    low = me[0] % (2 * LOW[0])
    hidden = wgate.shape[1] // 4
    fc = hidden // PARTS
    moves = [(attn_gain, gain1), (mlp_gain, gain2), (wq, qk.at[:, :d]), (wk, qk.at[:, d : 2 * d]),
             (wv, vo.at[:, :d]), (wo, vo.at[:, d:])]
    for ref, flip in ((keep, 0), (send, LOW[0])):
        for i, other in enumerate((0, LOW[1])):
            base = (low ^ (flip + other)) * hidden
            for c in range(PARTS):
                for m, w in enumerate((wgate, wup, wdown)):
                    at = i * 3 * hidden + (c * 3 + m) * fc
                    moves.append((w.at[:, pl.ds(pl.multiple_of(base + c * fc, 128), fc)], ref.at[:, at : at + fc]))
    copies = [pltpu.make_async_copy(src, dst, sems.at[i]) for i, (src, dst) in enumerate(moves)]
    for copy in copies:
        copy.start()
    for copy in copies[:2]:
        copy.wait()
    lane = lax.broadcasted_iota(jnp.int32, (rows, 128), 1)
    both = jnp.where(lane == 0, column_of(gain1[...]), jnp.where(lane == 1, column_of(gain2[...]), 0.0))
    qk[:, 2 * d :] = both.astype(bf16)
    for copy in copies[2:]:
        copy.wait()


def unpack_kernel(me, *refs):
    parts, outs = [ref.at[i] for ref in refs[:2] for i in range(2)], refs[2:]
    low = me[0] % (2 * LOW[0])
    hidden = outs[0].shape[1] // 4
    fc = hidden // PARTS
    for ref, flip in zip(parts, (0, LOW[1], LOW[0], LOW[0] + LOW[1])):
        base = (low ^ flip) * hidden
        for c in range(PARTS):
            for m, out in enumerate(outs):
                at = (c * 3 + m) * fc
                out[:, pl.ds(pl.multiple_of(base + c * fc, 128), fc)] = ref[:, at : at + fc].astype(f32)


def prep_kernel(me, tokens, cot, places, seq, cosine, sine, xp, gb, gbg, own_sel, group_sel, change, cos, sin):
    d = tokens.shape[1]
    rows = places[4, 0]
    share = 2 * LOW[0]
    own = (places[0:1] ^ me[0]) * rows + places[1:2]
    group = (places[2:3] ^ (me[0] - me[0] % share)) * rows + places[3:4]
    source = lax.broadcasted_iota(jnp.int32, (d, d), 0)
    own_sel[...] = (source == own).astype(bf16)
    group_sel[...] = (source == group).astype(bf16)
    own_col = jnp.broadcast_to(own.astype(f32), (128, d)).T[:, 0:1]
    change[...] = (own_col == group.astype(f32)).astype(bf16)
    xp[...] = nn(tokens[...], own_sel[...]).astype(bf16)
    live = (column_of(seq[...]) >= 0.0).astype(f32)
    gb[...] = (nn(cot[...], own_sel[...]) * live).astype(bf16)
    gbg[...] = (nn(cot[...], group_sel[...]) * live).astype(bf16)
    c, z = cosine[...], sine[...]
    cos[...] = jnp.concatenate([c, c, c, c], axis=1)
    sin[...] = jnp.concatenate([-z, z, -z, z], axis=1)


def fold_kernel(me, kept, got, keep, send):
    b = (me[0] // LOW[0]) % 2
    half = keep.shape[2]
    for at, ref in ((b, kept), (1 - b, got)):
        keep[pl.ds(at, 1)] = ref[:, :half][None]
        send[pl.ds(at, 1)] = ref[:, half:][None]


def fold2_kernel(me, kept, got, *parts):
    b = me[0] % 2
    cols = parts[0].shape[3]
    for c, out in enumerate(parts):
        for at, ref in ((b, kept), (1 - b, got)):
            out[pl.ds(at, 1)] = ref[:, :, c * cols : (c + 1) * cols][None]


def unfold_kernel(me, *refs):
    terms, (keep, send) = refs[:-2], refs[-2:]
    b = me[0] % 2
    cols = terms[0].shape[3]
    for c in range(PARTS):
        for at, ref in ((b, keep), (1 - b, send)):
            total = sum(v[pl.ds(at, 1)].astype(f32) for v in terms[2 * c : 2 * c + 2])
            ref[:, :, c * cols : (c + 1) * cols] = total[0].astype(bf16)


def unfold2_kernel(me, kept, got, keep, send):
    b = (me[0] // LOW[0]) % 2
    for i, ref in enumerate((kept, got)):
        keep[i : i + 1] = ref[pl.ds(b, 1)]
        send[i : i + 1] = ref[pl.ds(1 - b, 1)]


def attn_kernel(xp, qk0, qk1, vo0, vo1, cos, sin, seq_row, n1t, qr, kr, vb, ob, gains, n1):
    d = xp.shape[1]
    qk, vo = (qk0, qk1), (vo0, vo1)
    gt = jnp.concatenate([p[:, 2 * d :] for p in qk], axis=0).astype(f32).T
    gains[...] = gt[0:8]
    x = xp[...].astype(f32)
    r1 = lax.rsqrt(jnp.mean(x * x, axis=-1, keepdims=True) + EPS)
    normed = x * r1 * gt[0:1]
    n1[...] = normed.astype(bf16)
    n1t[...] = normed.T.astype(bf16)
    allowed = allowed_of(seq_row)
    pair = 2 * HD
    low = lax.broadcasted_iota(jnp.int32, (x.shape[0], pair), 1) < HD
    scale = HD ** -0.5
    for b in range(d // 256):
        cols = slice(b * 256, (b + 1) * 256)
        q2 = split_nn(n1, qk, cols)
        k2 = split_nn(n1, qk, slice(d + b * 256, d + (b + 1) * 256))
        vb[:, cols] = split_nn(n1, vo, cols).astype(bf16)
        for h in range(2):
            here = slice(h * pair, (h + 1) * pair)
            there = slice(b * 256 + h * pair, b * 256 + (h + 1) * pair)
            q, k = q2[:, here], k2[:, here]
            qr[:, there] = (q * cos[...] + swap_halves(q) * sin[...]).astype(bf16)
            kr[:, there] = (k * cos[...] + swap_halves(k) * sin[...]).astype(bf16)
    for b in range(d // pair):
        cols = slice(b * pair, (b + 1) * pair)
        q, k, v = qr[:, cols], kr[:, cols], vb[:, cols]
        outs = []
        for mine in (low, ~low):
            s = nt(jnp.where(mine, q, jnp.zeros_like(q)), k)
            logits = jnp.where(allowed, s * scale, MASKED)
            e = jnp.exp(logits - jnp.max(logits, axis=-1, keepdims=True))
            p = e / jnp.sum(e, axis=-1, keepdims=True)
            outs.append(nn(p.astype(bf16), v))
        ob[:, cols] = jnp.where(low, outs[0], outs[1]).astype(bf16)


def mid_kernel(xp, ob, vo0, vo1, gains, change, hmid, n2g):
    d = xp.shape[1]
    h = xp[...].astype(f32) + split_nt(ob[...], (vo0, vo1), slice(d, 2 * d))
    hmid[...] = h
    r2 = lax.rsqrt(jnp.mean(h * h, axis=-1, keepdims=True) + EPS)
    n2g[...] = nn((h * r2 * gains[1:2]).astype(bf16), change[...]).astype(bf16)


def ff_kernel(*refs):
    pieces, ws, (act, both, keep, send, n2, gb, acc) = refs[:8], refs[8 : 8 + PARTS], refs[8 + PARTS :]
    rows = pieces[0].shape[0]
    for i in range(4):
        n2[i * rows : (i + 1) * rows] = pieces[i][...]
        gb[i * rows : (i + 1) * rows] = pieces[4 + i][...]
    half = n2.shape[0] // 2
    for c, w in enumerate(ws):
        fc = w.shape[1] // 3
        gate = nn(n2[...], w[:, :fc])
        up = nn(n2[...], w[:, fc : 2 * fc])
        dact = nn(gb[...], w[:, 2 * fc :])
        sig = jax.nn.sigmoid(gate)
        silu = gate * sig
        act[:, c * fc : (c + 1) * fc] = (silu * up).astype(bf16)
        at = 2 * c * fc
        both[:, at : at + fc] = (dact * up * sig * (1.0 + gate * (1.0 - sig))).astype(bf16)
        both[:, at + fc : at + 2 * fc] = (dact * silu).astype(bf16)
        part = nt(both[:, at : at + 2 * fc], w[:, : 2 * fc])
        acc[...] = part if c == 0 else acc[...] + part
    keep[...] = acc[:half].astype(bf16)
    send[...] = acc[half:].astype(bf16)


def ff_grad_kernel(*refs):
    pieces, act, both, (n2t, gbt) = refs[:8], refs[8], refs[9], refs[-2:]
    rows = pieces[0].shape[0]
    for i in range(4):
        n2t[:, i * rows : (i + 1) * rows] = pieces[i][...].astype(f32).T.astype(bf16)
        gbt[:, i * rows : (i + 1) * rows] = pieces[4 + i][...].astype(f32).T.astype(bf16)
    refs = refs[10:-2]
    for c in range(PARTS):
        keep, send = refs[2 * c : 2 * c + 2]
        fc = keep.shape[1] // 3
        runs = 2 ** c
        run = n2t.shape[0] // (2 * runs)
        for left, right, cols in (
            (n2t, both[:, 2 * c * fc : 2 * (c + 1) * fc], slice(0, 2 * fc)),
            (gbt, act[:, c * fc : (c + 1) * fc], slice(2 * fc, 3 * fc)),
        ):
            dw = nn(left[...], right).astype(bf16)
            for r in range(runs):
                keep[r * run : (r + 1) * run, cols] = dw[2 * r * run : (2 * r + 1) * run]
                send[r * run : (r + 1) * run, cols] = dw[(2 * r + 1) * run : (2 * r + 2) * run]


def ff_out_kernel(act, *refs):
    ws, (keep, send) = refs[:PARTS], refs[PARTS:]
    half = act.shape[0] // 2
    fc = ws[0].shape[1] // 3
    for ref, rows in ((keep, slice(0, half)), (send, slice(half, 2 * half))):
        ref[...] = sum(nt(act[rows, c * fc : (c + 1) * fc], w[:, 2 * fc :]) for c, w in enumerate(ws)).astype(bf16)


def back_kernel(k1, g1, g2, hmid, gb, gains, vo0, vo1, ob, change, dh, dob, keep, send, dgain):
    t, d = hmid.shape
    half = d // 2
    total = k1[:t].astype(f32) + g1[:t].astype(f32) + g2[...].astype(f32)
    dn2 = moved(nt, total, change[...])
    h = hmid[...]
    r2 = lax.rsqrt(jnp.mean(h * h, axis=-1, keepdims=True) + EPS)
    dgain[...] = jnp.broadcast_to(jnp.sum(dn2 * h * r2, axis=0, keepdims=True), dgain.shape)
    dn2 = dn2 * gains[1:2]
    out = gb[...].astype(f32) + r2 * dn2 - h * (r2 * r2 * r2) * jnp.mean(dn2 * h, axis=-1, keepdims=True)
    dh[...] = out
    dob[...] = split_nn(out.astype(bf16), (vo0, vo1), slice(d, 2 * d)).astype(bf16)
    dw = nn(out.T.astype(bf16), ob[...]).astype(bf16)
    keep[...] = dw[:half]
    send[...] = dw[half:]


def attn_back_kernel(qr, kr, vb, dob, n1t, cos, sin, seq_row, dq, dk, dv, keep, send):
    t, d = qr.shape
    half = d // 2
    pair = 2 * HD
    allowed = allowed_of(seq_row)
    low = lax.broadcasted_iota(jnp.int32, (t, pair), 1) < HD
    scale = HD ** -0.5
    for b in range(d // pair):
        cols = slice(b * pair, (b + 1) * pair)
        q, k, v, do = qr[:, cols], kr[:, cols], vb[:, cols], dob[:, cols]
        dqs, dks, dvs = [], [], []
        for mine in (low, ~low):
            s = nt(jnp.where(mine, q, jnp.zeros_like(q)), k)
            logits = jnp.where(allowed, s * scale, MASKED)
            e = jnp.exp(logits - jnp.max(logits, axis=-1, keepdims=True))
            p = e / jnp.sum(e, axis=-1, keepdims=True)
            dp = nt(jnp.where(mine, do, jnp.zeros_like(do)), v)
            dlogit = p * (dp - jnp.sum(dp * p, axis=-1, keepdims=True))
            ds = jnp.where(allowed, dlogit * scale, 0.0)
            dvs.append(nn(p.T.astype(bf16), do))
            dqs.append(nn(ds.astype(bf16), k))
            dks.append(nn(ds.T.astype(bf16), q))
        dv[:, cols] = jnp.where(low, dvs[0], dvs[1]).astype(bf16)
        for grads, ref in ((dqs, dq), (dks, dk)):
            g = jnp.where(low, grads[0], grads[1])
            ref[:, cols] = (g * cos[...] - swap_halves(g) * sin[...]).astype(bf16)
    for part, ref in enumerate((dv, dq)):
        for b in range(d // 256):
            dw = nn(n1t[...], ref[:, b * 256 : (b + 1) * 256]).astype(bf16)
            cols = slice(part * d + b * 256, part * d + (b + 1) * 256)
            keep[:, cols] = dw[:half]
            send[:, cols] = dw[half:]


def last_kernel(dq, dk, dv, qk0, qk1, vo0, vo1, n1t, xp, dh, gains, dgain2, own_sel, dtok, keep, send):
    _, d = xp.shape
    half = d // 2
    qk, vo = (qk0, qk1), (vo0, vo1)
    dn1 = (split_nt(dq[...], qk, slice(0, d)) + split_nt(dk[...], qk, slice(d, 2 * d))
           + split_nt(dv[...], vo, slice(0, d)))
    dw = nn(n1t[...], dk[...]).astype(bf16)
    keep[:, :d] = dw[:half]
    send[:, :d] = dw[half:]
    x = xp[...].astype(f32)
    r1 = lax.rsqrt(jnp.mean(x * x, axis=-1, keepdims=True) + EPS)
    dgain1 = jnp.sum(dn1 * x * r1, axis=0, keepdims=True)
    row = lax.broadcasted_iota(jnp.int32, (128, d), 0)
    both = jnp.where(row == 0, dgain1, jnp.where(row == 1, dgain2[0:1], 0.0)).T.astype(bf16)
    keep[:, d:] = both[:half]
    send[:, d:] = both[half:]
    g = dn1 * gains[0:1]
    out = dh[...] + r1 * g - x * (r1 * r1 * r1) * jnp.mean(g * x, axis=-1, keepdims=True)
    dtok[...] = nt(out.astype(bf16), own_sel[...]).astype(bf16)


def out_kernel(k1, g1, g2, hmid, own_sel, group_sel, out):
    t = hmid.shape[0]
    total = k1[:t].astype(f32) + g1[:t].astype(f32) + g2[...].astype(f32)
    out[...] = (moved(nt, total, group_sel[...]) + moved(nt, hmid[...], own_sel[...])).astype(bf16)


def make_on_device(n):
    first, second = gather_orders(n)
    axis_bits = tuple(reversed(first))
    axis_of = {b: i for i, b in enumerate(axis_bits)}
    k = len(axis_bits)
    assert axis_bits[0] == first[-1] == second[-1]
    high = sorted((b for b in first if b not in LOW), reverse=True)
    ff_orders = (tuple(high), (high[-1],) + tuple(high[:-1]))
    ff_bits = tuple(reversed(high)) + tuple(reversed(LOW))
    ff_axis = {b: i for i, b in enumerate(ff_bits)}

    def swap(a, b):
        return lax.ppermute(a, "dp", [(i, i ^ b) for i in range(n)])

    def gather(shard, order):
        a = shard.reshape((1,) * k + shard.shape)
        for i, b in enumerate(order):
            got = swap(a, b)
            if i == k - 1:
                return tuple(v.reshape((n * shard.shape[0] // 2,) + shard.shape[1:]) for v in (a, got))
            a = jnp.concatenate([a, got], axis=axis_of[b])

    def reduce(keep, send, steps, axis, last):
        for i, b in enumerate(steps):
            got = swap(send, b)
            if i == len(steps) - 1:
                return (keep.astype(f32) + got.astype(f32)).astype(last) if last else (keep, got)
            ax = axis[steps[i + 1]]
            part = lambda v, at: lax.slice_in_dim(v, at, at + 1, axis=ax).astype(f32)
            send, keep = (
                (part(keep, 1) + part(got, 1)).astype(bf16),
                (part(keep, 0) + part(got, 0)).astype(bf16),
            )

    def scatter(keep, send, order):
        rows, cols = keep.shape[0] * 2 // n, keep.shape[1]
        shape = (1,) + (2,) * (k - 1) + (rows, cols)
        a = reduce(keep.reshape(shape), send.reshape(shape), tuple(reversed(order)), axis_of, f32)
        return a.reshape(rows, cols)

    def on_device(tokens, seq_ids, positions, cotangent, attn_gain, w_query, w_key, w_value, w_output,
                  mlp_gain, w_gate, w_up, w_down):
        toks, d = tokens.shape
        rows = d // n
        ff = w_gate.shape[1]
        share = 2 ** len(LOW)
        fc = ff // share // PARTS
        half = d // 2
        me = lax.axis_index("dp")

        def places_of(bits):
            slot = np.arange(d) // rows
            return sum(((slot >> (k - 1 - i)) & 1) * b for i, b in enumerate(bits)), np.arange(d) % rows

        places = jnp.asarray(np.stack([*places_of(axis_bits), *places_of(ff_bits), np.full(d, rows)]), jnp.int32)
        me1 = me[None]
        shards = [((rows, 2 * d + 128), bf16), ((rows, 2 * d), bf16)] + [((rows, 2 * ff * 3 // share), bf16)] * 2
        part_qk, part_vo, keep, send = call(
            pack_kernel, shards, me1, attn_gain[None, :], mlp_gain[None, :], w_query, w_key, w_value, w_output.T,
            w_gate, w_up, w_down.T, fetch=False, grant=3 * VMEM,
            scratch_shapes=[pltpu.VMEM((1, rows), bf16)] * 2 + [pltpu.SemaphoreType.DMA((6 + 12 * PARTS,))])
        mine = ff * 3 // share
        block = ((2, rows, mine), bf16)
        keep, send = call(fold_kernel, [block] * 2, me1, keep, swap(send, LOW[0]))
        ws = call(fold2_kernel, [((2, 2, rows, 3 * fc), bf16)] * PARTS, me1, keep, swap(send, LOW[1]))
        qk = gather(part_qk, first)
        vo = gather(part_vo, second)
        wff = []
        for c in range(PARTS):
            w = ws[c].reshape((1,) * len(high) + (2, 2, rows, 3 * fc))
            for b in ff_orders[c]:
                got = swap(w, b)
                w = jnp.concatenate([w, got], axis=ff_axis[b])
            wff.append(w.reshape(d, 3 * fc))
        freq = jnp.exp(jnp.arange(HD // 2, dtype=f32) * (-2.0 * math.log(THETA) / HD))
        angles = positions.astype(f32)[:, None] * freq[None, :]
        cosine, sine = jnp.cos(angles), jnp.sin(angles)
        seq_row = seq_ids[None, :]
        act, mat, wide = ((toks, d), bf16), ((d, toks), bf16), ((toks, d), f32)

        def group_gather(v):
            far = swap(v, LOW[0])
            near = swap(v, LOW[1])
            return v, far, near, swap(far, LOW[1])

        def group_halve(keep, send):
            g1 = swap(send, LOW[1])
            v = (keep[toks:].astype(f32) + g1[toks:].astype(f32)).astype(bf16)
            return keep, g1, swap(v, LOW[0])

        square, table = ((d, d), bf16), ((toks, 2 * HD), f32)
        xp, gb, gbg, own_sel, group_sel, change, cos2, sin2 = call(
            prep_kernel, [act] * 3 + [square] * 3 + [table] * 2, me1, tokens, cotangent, places, seq_row, cosine, sine)
        gb4 = group_gather(gbg)
        n1t, qr, kr, vb, ob, gains, _ = call(
            attn_kernel, [mat, act, act, act, act, ((8, d), f32), act],
            xp, *qk, *vo, cos2, sin2, seq_row)
        hmid, n2g = call(mid_kernel, [wide, act], xp, ob, *vo, gains, change)
        n24 = group_gather(n2g)
        tg = share * toks
        hidden = PARTS * fc
        pairs = [((tg // 2, d), bf16)] * 2
        acts, both, keep, send = call(
            ff_kernel, [((tg, hidden), bf16), ((tg, 2 * hidden), bf16)] + pairs, *n24, *gb4, *wff,
            scratch_shapes=[pltpu.VMEM((tg, d), bf16)] * 2 + [pltpu.VMEM((tg, d), f32)])
        dn2 = group_halve(keep, send)
        grads = call(
            ff_grad_kernel, [((half, 3 * fc), bf16)] * (2 * PARTS), *n24, *gb4, acts, both,
            scratch_shapes=[pltpu.VMEM((d, tg), bf16)] * 2)
        y = group_halve(*call(ff_out_kernel, pairs, acts, *wff))
        parts = []
        for c in range(PARTS):
            steps = tuple(reversed(ff_orders[c]))
            shape = tuple(1 if b == steps[0] else 2 for b in ff_bits) + (rows, 3 * fc)
            parts.append(reduce(*(v.reshape(shape) for v in grads[2 * c : 2 * c + 2]), steps, ff_axis, None))
        terms = [v.reshape(2, 2, rows, 3 * fc) for pair in parts for v in pair]
        keep, send = call(unfold_kernel, [block] * 2, me1, *terms)
        keep, send = call(unfold2_kernel, [block] * 2, me1, keep, swap(send, LOW[1]))
        got = swap(send, LOW[0])
        d_gate, d_up, d_down = call(
            unpack_kernel, [((rows, ff), f32)] * 3, me1, keep, got)
        dh, dob, keep, send, dgain2 = call(
            back_kernel, [wide, act, ((half, d), bf16), ((half, d), bf16), ((8, d), f32)],
            *dn2, hmid, gb, gains, *vo, ob, change)
        d_wo = scatter(keep, send, second)
        dq, dk, dv, keep, send = call(
            attn_back_kernel, [act, act, act, ((half, 2 * d), bf16), ((half, 2 * d), bf16)],
            qr, kr, vb, dob, n1t, cos2, sin2, seq_row)
        d_vq = scatter(keep, send, first)
        dtok, keep, send = call(
            last_kernel, [act, ((half, d + 128), bf16), ((half, d + 128), bf16)],
            dq, dk, dv, *qk, *vo, n1t, xp, dh, gains, dgain2, own_sel)
        d_kg = scatter(keep, send, second)
        (out,) = call(out_kernel, [act], *y, hmid, own_sel, group_sel)
        ends = (d_kg[:, d], d_vq[:, d:], d_kg[:, :d], d_vq[:, :d], d_wo.T, d_kg[:, d + 1])
        return (out, dtok, *ends, d_gate, d_up, d_down.T)

    return on_device


def solution(mesh):
    rows, cols, vec = P("dp", None), P(None, "dp"), P("dp")
    in_specs = (rows, vec, vec, rows, vec, rows, rows, rows, cols, vec, rows, rows, cols)
    out_specs = (rows, rows, vec, rows, rows, rows, cols, vec, rows, rows, cols)
    n = mesh.shape["dp"]
    return jax.shard_map(make_on_device(n), mesh=mesh, in_specs=in_specs, out_specs=out_specs, check_vma=False)
```

```python
import math

import jax
import jax.numpy as jnp
import numpy as np
from jax import lax
from jax.experimental import pallas as pl
from jax.experimental.pallas import tpu as pltpu
from jax.sharding import PartitionSpec as P


HD = 64
LOW = (2, 1)
PARTS = 4


def cuts(hidden):
    return (0, hidden, 2 * hidden, 2 * hidden + hidden // 2, 3 * hidden)


VMEM = 24 * 2**20
EPS = 1e-05
MASKED = -1e30
THETA = 10000.0


f32 = jnp.float32
bf16 = jnp.bfloat16


def gather_orders(n):
    if n == 32:
        return (16, 8, 2, 4, 1), (16, 8, 4, 2, 1)
    bits = [1 << k for k in range(n.bit_length() - 1)]
    order = tuple(reversed(bits))
    return order, order


def nn(a, b):
    return jnp.dot(a, b, preferred_element_type=f32)


def nt(a, b):
    return lax.dot_general(a, b, (((1,), (1,)), ((), ())), preferred_element_type=f32)


def call(kernel, outs, *args, fetch=True, grant=VMEM, **kw):
    out_shape = [jax.ShapeDtypeStruct(s, d) for s, d in outs]
    vmem = pl.BlockSpec(memory_space=pltpu.VMEM)
    smem = pl.BlockSpec(memory_space=pltpu.SMEM)
    hbm = pl.BlockSpec(memory_space=pltpu.HBM)
    return pl.pallas_call(
        kernel,
        out_shape=out_shape,
        in_specs=[smem if v.size == 1 else vmem if fetch else hbm for v in args],
        out_specs=[vmem] * len(outs),
        compiler_params=pltpu.CompilerParams(vmem_limit_bytes=grant),
        **kw,
    )(*args)


def moved(f, v, select):
    high = v.astype(bf16)
    return f(high, select) + f((v - high.astype(f32)).astype(bf16), select)


def split_nn(v, parts, cols):
    half = parts[0].shape[0]
    return nn(v[:, :half], parts[0][:, cols]) + nn(v[:, half:], parts[1][:, cols])


def split_nt(v, parts, cols):
    return jnp.concatenate([nt(v, p[:, cols]) for p in parts], axis=1)


def column_of(row):
    t = row.shape[1]
    i = lax.broadcasted_iota(jnp.int32, (t, t), 0)
    j = lax.broadcasted_iota(jnp.int32, (t, t), 1)
    return jnp.sum(jnp.where(i == j, row.astype(f32), 0.0), axis=1, keepdims=True)


def allowed_of(seq_ref):
    row = seq_ref[...].astype(f32)
    col = column_of(row)
    t = row.shape[1]
    i = lax.broadcasted_iota(jnp.int32, (t, t), 0)
    j = lax.broadcasted_iota(jnp.int32, (t, t), 1)
    return ((col == row) & (col >= 0.0) & (j <= i)) | (i == j)


def swap_halves(v):
    lane = lax.broadcasted_iota(jnp.int32, v.shape, 1)
    first = (lane % HD) < (HD // 2)
    return jnp.where(first, pltpu.roll(v, 2 * HD - HD // 2, 1), pltpu.roll(v, HD // 2, 1))


def pack_kernel(me, attn_gain, mlp_gain, wq, wk, wv, wo, wgate, wup, wdown, qk, vo, keep, send, gain1, gain2, sems):
    rows, d = wq.shape
    low = me[0] % (2 * LOW[0])
    hidden = wgate.shape[1] // 4
    moves = [(attn_gain, gain1), (mlp_gain, gain2), (wq, qk.at[:, :d]), (wk, qk.at[:, d : 2 * d]),
             (wv, vo.at[:, :d]), (wo, vo.at[:, d:])]
    for ref, flip in ((keep, 0), (send, LOW[0])):
        for i, other in enumerate((0, LOW[1])):
            base = (low ^ (flip + other)) * hidden
            for m, w in enumerate((wgate, wup, wdown)):
                at = (i * 3 + m) * hidden
                moves.append((w.at[:, pl.ds(pl.multiple_of(base, 128), hidden)], ref.at[:, at : at + hidden]))
    copies = [pltpu.make_async_copy(src, dst, sems.at[i]) for i, (src, dst) in enumerate(moves)]
    for copy in copies:
        copy.start()
    for copy in copies[:2]:
        copy.wait()
    lane = lax.broadcasted_iota(jnp.int32, (rows, 128), 1)
    both = jnp.where(lane == 0, column_of(gain1[...]), jnp.where(lane == 1, column_of(gain2[...]), 0.0))
    qk[:, 2 * d :] = both.astype(bf16)
    for copy in copies[2:]:
        copy.wait()


def unpack_kernel(me, *refs):
    parts, outs = [ref.at[i] for ref in refs[:2] for i in range(2)], refs[2:]
    low = me[0] % (2 * LOW[0])
    hidden = outs[0].shape[1] // 4
    for ref, flip in zip(parts, (0, LOW[1], LOW[0], LOW[0] + LOW[1])):
        base = (low ^ flip) * hidden
        for m, out in enumerate(outs):
            out[:, pl.ds(pl.multiple_of(base, 128), hidden)] = ref[:, m * hidden : (m + 1) * hidden].astype(f32)


def prep_kernel(me, tokens, cot, places, seq, cosine, sine, xp, gb, gbg, own_sel, group_sel, change, cos, sin):
    d = tokens.shape[1]
    rows = places[4, 0]
    share = 2 * LOW[0]
    own = (places[0:1] ^ me[0]) * rows + places[1:2]
    group = (places[2:3] ^ (me[0] - me[0] % share)) * rows + places[3:4]
    source = lax.broadcasted_iota(jnp.int32, (d, d), 0)
    own_sel[...] = (source == own).astype(bf16)
    group_sel[...] = (source == group).astype(bf16)
    own_col = jnp.broadcast_to(own.astype(f32), (128, d)).T[:, 0:1]
    change[...] = (own_col == group.astype(f32)).astype(bf16)
    xp[...] = nn(tokens[...], own_sel[...]).astype(bf16)
    live = (column_of(seq[...]) >= 0.0).astype(f32)
    gb[...] = (nn(cot[...], own_sel[...]) * live).astype(bf16)
    gbg[...] = (nn(cot[...], group_sel[...]) * live).astype(bf16)
    c, z = cosine[...], sine[...]
    cos[...] = jnp.concatenate([c, c, c, c], axis=1)
    sin[...] = jnp.concatenate([-z, z, -z, z], axis=1)


def fold_kernel(me, kept, got, keep, send):
    b = (me[0] // LOW[0]) % 2
    half = keep.shape[2]
    for at, ref in ((b, kept), (1 - b, got)):
        keep[pl.ds(at, 1)] = ref[:, :half][None]
        send[pl.ds(at, 1)] = ref[:, half:][None]


def fold2_kernel(me, kept, got, *parts):
    b = me[0] % 2
    edges = cuts(kept.shape[2] // 3)
    for c, out in enumerate(parts):
        for at, ref in ((b, kept), (1 - b, got)):
            out[pl.ds(at, 1)] = ref[:, :, edges[c] : edges[c + 1]][None]


def unfold_kernel(me, *refs):
    terms, (keep, send) = refs[:-2], refs[-2:]
    b = me[0] % 2
    edges = cuts(keep.shape[2] // 3)
    for c in range(PARTS):
        for at, ref in ((b, keep), (1 - b, send)):
            total = sum(v[pl.ds(at, 1)].astype(f32) for v in terms[2 * c : 2 * c + 2])
            ref[:, :, edges[c] : edges[c + 1]] = total[0].astype(bf16)


def unfold2_kernel(me, kept, got, keep, send):
    b = (me[0] // LOW[0]) % 2
    for i, ref in enumerate((kept, got)):
        keep[i : i + 1] = ref[pl.ds(b, 1)]
        send[i : i + 1] = ref[pl.ds(1 - b, 1)]


def attn_kernel(xp, qk0, qk1, vo0, vo1, cos, sin, seq_row, n1t, qr, kr, vb, ob, gains, n1):
    d = xp.shape[1]
    qk, vo = (qk0, qk1), (vo0, vo1)
    gt = jnp.concatenate([p[:, 2 * d :] for p in qk], axis=0).astype(f32).T
    gains[...] = gt[0:8]
    x = xp[...].astype(f32)
    r1 = lax.rsqrt(jnp.mean(x * x, axis=-1, keepdims=True) + EPS)
    normed = x * r1 * gt[0:1]
    n1[...] = normed.astype(bf16)
    n1t[...] = normed.T.astype(bf16)
    allowed = allowed_of(seq_row)
    pair = 2 * HD
    low = lax.broadcasted_iota(jnp.int32, (x.shape[0], pair), 1) < HD
    scale = HD ** -0.5
    for b in range(d // 256):
        cols = slice(b * 256, (b + 1) * 256)
        q2 = split_nn(n1, qk, cols)
        k2 = split_nn(n1, qk, slice(d + b * 256, d + (b + 1) * 256))
        vb[:, cols] = split_nn(n1, vo, cols).astype(bf16)
        for h in range(2):
            here = slice(h * pair, (h + 1) * pair)
            there = slice(b * 256 + h * pair, b * 256 + (h + 1) * pair)
            q, k = q2[:, here], k2[:, here]
            qr[:, there] = (q * cos[...] + swap_halves(q) * sin[...]).astype(bf16)
            kr[:, there] = (k * cos[...] + swap_halves(k) * sin[...]).astype(bf16)
    for b in range(d // pair):
        cols = slice(b * pair, (b + 1) * pair)
        q, k, v = qr[:, cols], kr[:, cols], vb[:, cols]
        outs = []
        for mine in (low, ~low):
            s = nt(jnp.where(mine, q, jnp.zeros_like(q)), k)
            logits = jnp.where(allowed, s * scale, MASKED)
            e = jnp.exp(logits - jnp.max(logits, axis=-1, keepdims=True))
            p = e / jnp.sum(e, axis=-1, keepdims=True)
            outs.append(nn(p.astype(bf16), v))
        ob[:, cols] = jnp.where(low, outs[0], outs[1]).astype(bf16)


def mid_kernel(xp, ob, vo0, vo1, gains, change, hmid, n2g):
    d = xp.shape[1]
    h = xp[...].astype(f32) + split_nt(ob[...], (vo0, vo1), slice(d, 2 * d))
    hmid[...] = h
    r2 = lax.rsqrt(jnp.mean(h * h, axis=-1, keepdims=True) + EPS)
    n2g[...] = nn((h * r2 * gains[1:2]).astype(bf16), change[...]).astype(bf16)


def ff_kernel(*refs):
    pieces, (wg, wu, *wd), (act, dg, du, keep, send, n2, gb, acc) = refs[:8], refs[8:12], refs[12:]
    rows = pieces[0].shape[0]
    for i in range(4):
        n2[i * rows : (i + 1) * rows] = pieces[i][...]
        gb[i * rows : (i + 1) * rows] = pieces[4 + i][...]
    half = n2.shape[0] // 2
    fc = wd[0].shape[1]
    for c in range(2):
        cols = slice(c * fc, (c + 1) * fc)
        gate = nn(n2[...], wg[:, cols])
        up = nn(n2[...], wu[:, cols])
        dact = nn(gb[...], wd[c][...])
        sig = jax.nn.sigmoid(gate)
        silu = gate * sig
        act[:, cols] = (silu * up).astype(bf16)
        dg[:, cols] = (dact * up * sig * (1.0 + gate * (1.0 - sig))).astype(bf16)
        du[:, cols] = (dact * silu).astype(bf16)
        part = nt(dg[:, cols], wg[:, cols]) + nt(du[:, cols], wu[:, cols])
        acc[...] = part if c == 0 else acc[...] + part
    keep[...] = acc[:half].astype(bf16)
    send[...] = acc[half:].astype(bf16)


def ff_grad_kernel(*refs):
    pieces, (act, dg, du), sides, (n2t, gbt) = refs[:8], refs[8:11], refs[11:-2], refs[-2:]
    rows = pieces[0].shape[0]
    for i in range(4):
        n2t[:, i * rows : (i + 1) * rows] = pieces[i][...].astype(f32).T.astype(bf16)
        gbt[:, i * rows : (i + 1) * rows] = pieces[4 + i][...].astype(f32).T.astype(bf16)
    fc = act.shape[1] // 2
    for c, (left, right) in enumerate(((n2t, dg[...]), (n2t, du[...]), (gbt, act[:, :fc]), (gbt, act[:, fc:]))):
        keep, send = sides[2 * c : 2 * c + 2]
        runs = 1 + c % 2
        run = n2t.shape[0] // (2 * runs)
        dw = nn(left[...], right).astype(bf16)
        for r in range(runs):
            keep[r * run : (r + 1) * run] = dw[2 * r * run : (2 * r + 1) * run]
            send[r * run : (r + 1) * run] = dw[(2 * r + 1) * run : (2 * r + 2) * run]


def ff_out_kernel(act, w0, w1, keep, send):
    half = act.shape[0] // 2
    fc = w0.shape[1]
    for ref, rows in ((keep, slice(0, half)), (send, slice(half, 2 * half))):
        ref[...] = (nt(act[rows, :fc], w0[...]) + nt(act[rows, fc:], w1[...])).astype(bf16)


def back_kernel(k1, g1, g2, hmid, gb, gains, vo0, vo1, ob, change, dh, dob, keep, send, dgain):
    t, d = hmid.shape
    half = d // 2
    total = k1[:t].astype(f32) + g1[:t].astype(f32) + g2[...].astype(f32)
    dn2 = moved(nt, total, change[...])
    h = hmid[...]
    r2 = lax.rsqrt(jnp.mean(h * h, axis=-1, keepdims=True) + EPS)
    dgain[...] = jnp.broadcast_to(jnp.sum(dn2 * h * r2, axis=0, keepdims=True), dgain.shape)
    dn2 = dn2 * gains[1:2]
    out = gb[...].astype(f32) + r2 * dn2 - h * (r2 * r2 * r2) * jnp.mean(dn2 * h, axis=-1, keepdims=True)
    dh[...] = out
    dob[...] = split_nn(out.astype(bf16), (vo0, vo1), slice(d, 2 * d)).astype(bf16)
    dw = nn(out.T.astype(bf16), ob[...]).astype(bf16)
    keep[...] = dw[:half]
    send[...] = dw[half:]


def attn_back_kernel(qr, kr, vb, dob, n1t, cos, sin, seq_row, dq, dk, dv, keep, send):
    t, d = qr.shape
    half = d // 2
    pair = 2 * HD
    allowed = allowed_of(seq_row)
    low = lax.broadcasted_iota(jnp.int32, (t, pair), 1) < HD
    scale = HD ** -0.5
    for b in range(d // pair):
        cols = slice(b * pair, (b + 1) * pair)
        q, k, v, do = qr[:, cols], kr[:, cols], vb[:, cols], dob[:, cols]
        dqs, dks, dvs = [], [], []
        for mine in (low, ~low):
            s = nt(jnp.where(mine, q, jnp.zeros_like(q)), k)
            logits = jnp.where(allowed, s * scale, MASKED)
            e = jnp.exp(logits - jnp.max(logits, axis=-1, keepdims=True))
            p = e / jnp.sum(e, axis=-1, keepdims=True)
            dp = nt(jnp.where(mine, do, jnp.zeros_like(do)), v)
            dlogit = p * (dp - jnp.sum(dp * p, axis=-1, keepdims=True))
            ds = jnp.where(allowed, dlogit * scale, 0.0)
            dvs.append(nn(p.T.astype(bf16), do))
            dqs.append(nn(ds.astype(bf16), k))
            dks.append(nn(ds.T.astype(bf16), q))
        dv[:, cols] = jnp.where(low, dvs[0], dvs[1]).astype(bf16)
        for grads, ref in ((dqs, dq), (dks, dk)):
            g = jnp.where(low, grads[0], grads[1])
            ref[:, cols] = (g * cos[...] - swap_halves(g) * sin[...]).astype(bf16)
    for part, ref in enumerate((dv, dq)):
        for b in range(d // 256):
            dw = nn(n1t[...], ref[:, b * 256 : (b + 1) * 256]).astype(bf16)
            cols = slice(part * d + b * 256, part * d + (b + 1) * 256)
            keep[:, cols] = dw[:half]
            send[:, cols] = dw[half:]


def last_kernel(dq, dk, dv, qk0, qk1, vo0, vo1, n1t, xp, dh, gains, dgain2, own_sel, dtok, keep, send):
    _, d = xp.shape
    half = d // 2
    qk, vo = (qk0, qk1), (vo0, vo1)
    dn1 = (split_nt(dq[...], qk, slice(0, d)) + split_nt(dk[...], qk, slice(d, 2 * d))
           + split_nt(dv[...], vo, slice(0, d)))
    dw = nn(n1t[...], dk[...]).astype(bf16)
    keep[:, :d] = dw[:half]
    send[:, :d] = dw[half:]
    x = xp[...].astype(f32)
    r1 = lax.rsqrt(jnp.mean(x * x, axis=-1, keepdims=True) + EPS)
    dgain1 = jnp.sum(dn1 * x * r1, axis=0, keepdims=True)
    row = lax.broadcasted_iota(jnp.int32, (128, d), 0)
    both = jnp.where(row == 0, dgain1, jnp.where(row == 1, dgain2[0:1], 0.0)).T.astype(bf16)
    keep[:, d:] = both[:half]
    send[:, d:] = both[half:]
    g = dn1 * gains[0:1]
    out = dh[...] + r1 * g - x * (r1 * r1 * r1) * jnp.mean(g * x, axis=-1, keepdims=True)
    dtok[...] = nt(out.astype(bf16), own_sel[...]).astype(bf16)


def out_kernel(k1, g1, g2, hmid, own_sel, group_sel, out):
    t = hmid.shape[0]
    total = k1[:t].astype(f32) + g1[:t].astype(f32) + g2[...].astype(f32)
    out[...] = (moved(nt, total, group_sel[...]) + moved(nt, hmid[...], own_sel[...])).astype(bf16)


def make_on_device(n):
    first, second = gather_orders(n)
    axis_bits = tuple(reversed(first))
    axis_of = {b: i for i, b in enumerate(axis_bits)}
    k = len(axis_bits)
    assert axis_bits[0] == first[-1] == second[-1]
    high = sorted((b for b in first if b not in LOW), reverse=True)
    ff_orders = (tuple(high), (high[-1],) + tuple(high[:-1]))
    ff_bits = tuple(reversed(high)) + tuple(reversed(LOW))
    ff_axis = {b: i for i, b in enumerate(ff_bits)}

    def swap(a, b):
        return lax.ppermute(a, "dp", [(i, i ^ b) for i in range(n)])

    def gather(shard, order):
        a = shard.reshape((1,) * k + shard.shape)
        for i, b in enumerate(order):
            got = swap(a, b)
            if i == k - 1:
                return tuple(v.reshape((n * shard.shape[0] // 2,) + shard.shape[1:]) for v in (a, got))
            a = jnp.concatenate([a, got], axis=axis_of[b])

    def reduce(keep, send, steps, axis, last):
        for i, b in enumerate(steps):
            got = swap(send, b)
            if i == len(steps) - 1:
                return (keep.astype(f32) + got.astype(f32)).astype(last) if last else (keep, got)
            ax = axis[steps[i + 1]]
            part = lambda v, at: lax.slice_in_dim(v, at, at + 1, axis=ax).astype(f32)
            send, keep = (
                (part(keep, 1) + part(got, 1)).astype(bf16),
                (part(keep, 0) + part(got, 0)).astype(bf16),
            )

    def scatter(keep, send, order):
        rows, cols = keep.shape[0] * 2 // n, keep.shape[1]
        shape = (1,) + (2,) * (k - 1) + (rows, cols)
        a = reduce(keep.reshape(shape), send.reshape(shape), tuple(reversed(order)), axis_of, f32)
        return a.reshape(rows, cols)

    def on_device(tokens, seq_ids, positions, cotangent, attn_gain, w_query, w_key, w_value, w_output,
                  mlp_gain, w_gate, w_up, w_down):
        toks, d = tokens.shape
        rows = d // n
        ff = w_gate.shape[1]
        share = 2 ** len(LOW)
        hidden = ff // share
        edges = cuts(hidden)
        widths = [b - a for a, b in zip(edges, edges[1:])]
        half = d // 2
        me = lax.axis_index("dp")

        def places_of(bits):
            slot = np.arange(d) // rows
            return sum(((slot >> (k - 1 - i)) & 1) * b for i, b in enumerate(bits)), np.arange(d) % rows

        places = jnp.asarray(np.stack([*places_of(axis_bits), *places_of(ff_bits), np.full(d, rows)]), jnp.int32)
        me1 = me[None]
        shards = [((rows, 2 * d + 128), bf16), ((rows, 2 * d), bf16)] + [((rows, 2 * ff * 3 // share), bf16)] * 2
        part_qk, part_vo, keep, send = call(
            pack_kernel, shards, me1, attn_gain[None, :], mlp_gain[None, :], w_query, w_key, w_value, w_output.T,
            w_gate, w_up, w_down.T, fetch=False, grant=3 * VMEM,
            scratch_shapes=[pltpu.VMEM((1, rows), bf16)] * 2 + [pltpu.SemaphoreType.DMA((18,))])
        mine = ff * 3 // share
        block = ((2, rows, mine), bf16)
        keep, send = call(fold_kernel, [block] * 2, me1, keep, swap(send, LOW[0]))
        ws = call(fold2_kernel, [((2, 2, rows, v), bf16) for v in widths], me1, keep, swap(send, LOW[1]))
        qk = gather(part_qk, first)
        vo = gather(part_vo, second)
        wff = []
        for c in range(PARTS):
            w = ws[c].reshape((1,) * len(high) + (2, 2, rows, widths[c]))
            for b in ff_orders[c % 2]:
                got = swap(w, b)
                w = jnp.concatenate([w, got], axis=ff_axis[b])
            wff.append(w.reshape(d, widths[c]))
        freq = jnp.exp(jnp.arange(HD // 2, dtype=f32) * (-2.0 * math.log(THETA) / HD))
        angles = positions.astype(f32)[:, None] * freq[None, :]
        cosine, sine = jnp.cos(angles), jnp.sin(angles)
        seq_row = seq_ids[None, :]
        act, mat, wide = ((toks, d), bf16), ((d, toks), bf16), ((toks, d), f32)

        def group_gather(v):
            far = swap(v, LOW[0])
            near = swap(v, LOW[1])
            return v, far, near, swap(far, LOW[1])

        def group_halve(keep, send):
            g1 = swap(send, LOW[1])
            v = (keep[toks:].astype(f32) + g1[toks:].astype(f32)).astype(bf16)
            return keep, g1, swap(v, LOW[0])

        square, table = ((d, d), bf16), ((toks, 2 * HD), f32)
        xp, gb, gbg, own_sel, group_sel, change, cos2, sin2 = call(
            prep_kernel, [act] * 3 + [square] * 3 + [table] * 2, me1, tokens, cotangent, places, seq_row, cosine, sine)
        gb4 = group_gather(gbg)
        n1t, qr, kr, vb, ob, gains, _ = call(
            attn_kernel, [mat, act, act, act, act, ((8, d), f32), act],
            xp, *qk, *vo, cos2, sin2, seq_row)
        hmid, n2g = call(mid_kernel, [wide, act], xp, ob, *vo, gains, change)
        n24 = group_gather(n2g)
        tg = share * toks
        pairs = [((tg // 2, d), bf16)] * 2
        acts, dg, du, keep, send = call(
            ff_kernel, [((tg, hidden), bf16)] * 3 + pairs, *n24, *gb4, *wff,
            scratch_shapes=[pltpu.VMEM((tg, d), bf16)] * 2 + [pltpu.VMEM((tg, d), f32)])
        dn2 = group_halve(keep, send)
        grads = call(
            ff_grad_kernel, [((half, v), bf16) for v in widths for _ in range(2)], *n24, *gb4, acts, dg, du,
            scratch_shapes=[pltpu.VMEM((d, tg), bf16)] * 2)
        y = group_halve(*call(ff_out_kernel, pairs, acts, *wff[2:]))
        parts = []
        for c in range(PARTS):
            steps = tuple(reversed(ff_orders[c % 2]))
            shape = tuple(1 if b == steps[0] else 2 for b in ff_bits) + (rows, widths[c])
            parts.append(reduce(*(v.reshape(shape) for v in grads[2 * c : 2 * c + 2]), steps, ff_axis, None))
        terms = [v.reshape(2, 2, rows, -1) for pair in parts for v in pair]
        keep, send = call(unfold_kernel, [block] * 2, me1, *terms)
        keep, send = call(unfold2_kernel, [block] * 2, me1, keep, swap(send, LOW[1]))
        got = swap(send, LOW[0])
        d_gate, d_up, d_down = call(
            unpack_kernel, [((rows, ff), f32)] * 3, me1, keep, got)
        dh, dob, keep, send, dgain2 = call(
            back_kernel, [wide, act, ((half, d), bf16), ((half, d), bf16), ((8, d), f32)],
            *dn2, hmid, gb, gains, *vo, ob, change)
        d_wo = scatter(keep, send, second)
        dq, dk, dv, keep, send = call(
            attn_back_kernel, [act, act, act, ((half, 2 * d), bf16), ((half, 2 * d), bf16)],
            qr, kr, vb, dob, n1t, cos2, sin2, seq_row)
        d_vq = scatter(keep, send, first)
        dtok, keep, send = call(
            last_kernel, [act, ((half, d + 128), bf16), ((half, d + 128), bf16)],
            dq, dk, dv, *qk, *vo, n1t, xp, dh, gains, dgain2, own_sel)
        d_kg = scatter(keep, send, second)
        (out,) = call(out_kernel, [act], *y, hmid, own_sel, group_sel)
        ends = (d_kg[:, d], d_vq[:, d:], d_kg[:, :d], d_vq[:, :d], d_wo.T, d_kg[:, d + 1])
        return (out, dtok, *ends, d_gate, d_up, d_down.T)

    return on_device


def solution(mesh):
    rows, cols, vec = P("dp", None), P(None, "dp"), P("dp")
    in_specs = (rows, vec, vec, rows, vec, rows, rows, rows, cols, vec, rows, rows, cols)
    out_specs = (rows, rows, vec, rows, rows, rows, cols, vec, rows, rows, cols)
    n = mesh.shape["dp"]
    return jax.shard_map(make_on_device(n), mesh=mesh, in_specs=in_specs, out_specs=out_specs, check_vma=False)
```

```python
import math

import jax
import jax.numpy as jnp
import numpy as np
from jax import lax
from jax.experimental import pallas as pl
from jax.experimental.pallas import tpu as pltpu
from jax.sharding import PartitionSpec as P


H = 12
HD = 64
LOW = (2, 1)
PARTS = 4


def cuts(hidden):
    return (0, hidden, 2 * hidden, 2 * hidden + hidden // 2, 3 * hidden)


VMEM = 24 * 2**20
EPS = 1e-05
MASKED = -1e30
THETA = 10000.0


f32 = jnp.float32
bf16 = jnp.bfloat16


def gather_orders(n):
    if n == 32:
        return (16, 8, 2, 4, 1), (16, 8, 4, 2, 1)
    bits = [1 << k for k in range(n.bit_length() - 1)]
    order = tuple(reversed(bits))
    return order, order


def nn(a, b):
    return jnp.dot(a, b, preferred_element_type=f32)


def nt(a, b):
    return lax.dot_general(a, b, (((1,), (1,)), ((), ())), preferred_element_type=f32)


def call(kernel, outs, *args, fetch=True, grant=VMEM, **kw):
    out_shape = [jax.ShapeDtypeStruct(s, d) for s, d in outs]
    vmem = pl.BlockSpec(memory_space=pltpu.VMEM)
    smem = pl.BlockSpec(memory_space=pltpu.SMEM)
    hbm = pl.BlockSpec(memory_space=pltpu.HBM)
    return pl.pallas_call(
        kernel,
        out_shape=out_shape,
        in_specs=[smem if v.size == 1 else vmem if fetch else hbm for v in args],
        out_specs=[vmem] * len(outs),
        compiler_params=pltpu.CompilerParams(vmem_limit_bytes=grant),
        **kw,
    )(*args)


def moved(f, v, select):
    high = v.astype(bf16)
    return f(high, select) + f((v - high.astype(f32)).astype(bf16), select)


def split_nn(v, parts, cols):
    half = parts[0].shape[0]
    return nn(v[:, :half], parts[0][:, cols]) + nn(v[:, half:], parts[1][:, cols])


def split_nt(v, parts, cols):
    return jnp.concatenate([nt(v, p[:, cols]) for p in parts], axis=1)


def column_of(row):
    t = row.shape[1]
    i = lax.broadcasted_iota(jnp.int32, (t, t), 0)
    j = lax.broadcasted_iota(jnp.int32, (t, t), 1)
    return jnp.sum(jnp.where(i == j, row.astype(f32), 0.0), axis=1, keepdims=True)


def allowed_of(seq_ref):
    row = seq_ref[...].astype(f32)
    col = column_of(row)
    t = row.shape[1]
    i = lax.broadcasted_iota(jnp.int32, (t, t), 0)
    j = lax.broadcasted_iota(jnp.int32, (t, t), 1)
    return ((col == row) & (col >= 0.0) & (j <= i)) | (i == j)


def swap_halves(v):
    lane = lax.broadcasted_iota(jnp.int32, v.shape, 1)
    first = (lane % HD) < (HD // 2)
    return jnp.where(first, pltpu.roll(v, 2 * HD - HD // 2, 1), pltpu.roll(v, HD // 2, 1))


def pack_kernel(me, attn_gain, mlp_gain, wq, wk, wv, wo, wgate, wup, wdown, qk, vo, keep, send, gain1, gain2, sems):
    rows, d = wq.shape
    low = me[0] % (2 * LOW[0])
    hidden = wgate.shape[1] // 4
    moves = [(attn_gain, gain1), (mlp_gain, gain2), (wq, qk.at[:, :d]), (wk, qk.at[:, d : 2 * d]),
             (wv, vo.at[:, :d]), (wo, vo.at[:, d:])]
    for ref, flip in ((keep, 0), (send, LOW[0])):
        for i, other in enumerate((0, LOW[1])):
            base = (low ^ (flip + other)) * hidden
            for m, w in enumerate((wgate, wup, wdown)):
                at = (i * 3 + m) * hidden
                moves.append((w.at[:, pl.ds(pl.multiple_of(base, 128), hidden)], ref.at[:, at : at + hidden]))
    copies = [pltpu.make_async_copy(src, dst, sems.at[i]) for i, (src, dst) in enumerate(moves)]
    for copy in copies:
        copy.start()
    for copy in copies[:2]:
        copy.wait()
    lane = lax.broadcasted_iota(jnp.int32, (rows, 128), 1)
    both = jnp.where(lane == 0, column_of(gain1[...]), jnp.where(lane == 1, column_of(gain2[...]), 0.0))
    qk[:, 2 * d :] = both.astype(bf16)
    for copy in copies[2:]:
        copy.wait()


def unpack_kernel(me, *refs):
    parts, outs = [ref.at[i] for ref in refs[:2] for i in range(2)], refs[2:]
    low = me[0] % (2 * LOW[0])
    hidden = outs[0].shape[1] // 4
    for ref, flip in zip(parts, (0, LOW[1], LOW[0], LOW[0] + LOW[1])):
        base = (low ^ flip) * hidden
        for m, out in enumerate(outs):
            out[:, pl.ds(pl.multiple_of(base, 128), hidden)] = ref[:, m * hidden : (m + 1) * hidden].astype(f32)


def prep_kernel(me, tokens, cot, places, seq, cosine, sine, xp, gb, gbg, own_sel, group_sel, change, cos, sin):
    d = tokens.shape[1]
    rows = places[4, 0]
    share = 2 * LOW[0]
    own = (places[0:1] ^ me[0]) * rows + places[1:2]
    group = (places[2:3] ^ (me[0] - me[0] % share)) * rows + places[3:4]
    source = lax.broadcasted_iota(jnp.int32, (d, d), 0)
    own_sel[...] = (source == own).astype(bf16)
    group_sel[...] = (source == group).astype(bf16)
    own_col = jnp.broadcast_to(own.astype(f32), (128, d)).T[:, 0:1]
    change[...] = (own_col == group.astype(f32)).astype(bf16)
    xp[...] = nn(tokens[...], own_sel[...]).astype(bf16)
    live = (column_of(seq[...]) >= 0.0).astype(f32)
    gb[...] = (nn(cot[...], own_sel[...]) * live).astype(bf16)
    gbg[...] = (nn(cot[...], group_sel[...]) * live).astype(bf16)
    c, z = cosine[...], sine[...]
    cos[...] = jnp.concatenate([c, c, c, c], axis=1)
    sin[...] = jnp.concatenate([-z, z, -z, z], axis=1)


def fold_kernel(me, kept, got, keep, send):
    b = (me[0] // LOW[0]) % 2
    half = keep.shape[2]
    for at, ref in ((b, kept), (1 - b, got)):
        keep[pl.ds(at, 1)] = ref[:, :half][None]
        send[pl.ds(at, 1)] = ref[:, half:][None]


def fold2_kernel(me, kept, got, *parts):
    b = me[0] % 2
    edges = cuts(kept.shape[2] // 3)
    for c, out in enumerate(parts):
        for at, ref in ((b, kept), (1 - b, got)):
            out[pl.ds(at, 1)] = ref[:, :, edges[c] : edges[c + 1]][None]


def unfold_kernel(me, *refs):
    terms, (keep, send) = refs[:-2], refs[-2:]
    b = me[0] % 2
    edges = cuts(keep.shape[2] // 3)
    for c in range(PARTS):
        for at, ref in ((b, keep), (1 - b, send)):
            total = sum(v[pl.ds(at, 1)].astype(f32) for v in terms[2 * c : 2 * c + 2])
            ref[:, :, edges[c] : edges[c + 1]] = total[0].astype(bf16)


def unfold2_kernel(me, kept, got, keep, send):
    b = (me[0] // LOW[0]) % 2
    for i, ref in enumerate((kept, got)):
        keep[i : i + 1] = ref[pl.ds(b, 1)]
        send[i : i + 1] = ref[pl.ds(1 - b, 1)]


def attn_kernel(xp, qk0, qk1, vo0, vo1, cos, sin, seq_row, n1t, qr, kr, vb, ob, probs, gains, n1):
    d = xp.shape[1]
    qk, vo = (qk0, qk1), (vo0, vo1)
    gt = jnp.concatenate([p[:, 2 * d :] for p in qk], axis=0).astype(f32).T
    gains[...] = gt[0:8]
    x = xp[...].astype(f32)
    r1 = lax.rsqrt(jnp.mean(x * x, axis=-1, keepdims=True) + EPS)
    normed = x * r1 * gt[0:1]
    n1[...] = normed.astype(bf16)
    n1t[...] = normed.T.astype(bf16)
    allowed = allowed_of(seq_row)
    pair = 2 * HD
    low = lax.broadcasted_iota(jnp.int32, (x.shape[0], pair), 1) < HD
    scale = HD ** -0.5
    for b in range(d // 256):
        cols = slice(b * 256, (b + 1) * 256)
        q2 = split_nn(n1, qk, cols)
        k2 = split_nn(n1, qk, slice(d + b * 256, d + (b + 1) * 256))
        vb[:, cols] = split_nn(n1, vo, cols).astype(bf16)
        for h in range(2):
            here = slice(h * pair, (h + 1) * pair)
            there = slice(b * 256 + h * pair, b * 256 + (h + 1) * pair)
            q, k = q2[:, here], k2[:, here]
            qr[:, there] = (q * cos[...] + swap_halves(q) * sin[...]).astype(bf16)
            kr[:, there] = (k * cos[...] + swap_halves(k) * sin[...]).astype(bf16)
    for b in range(d // pair):
        cols = slice(b * pair, (b + 1) * pair)
        q, k, v = qr[:, cols], kr[:, cols], vb[:, cols]
        outs = []
        for h, mine in enumerate((low, ~low)):
            s = nt(jnp.where(mine, q, jnp.zeros_like(q)), k)
            logits = jnp.where(allowed, s * scale, MASKED)
            e = jnp.exp(logits - jnp.max(logits, axis=-1, keepdims=True))
            p = e / jnp.sum(e, axis=-1, keepdims=True)
            probs[2 * b + h] = p
            outs.append(nn(p.astype(bf16), v))
        ob[:, cols] = jnp.where(low, outs[0], outs[1]).astype(bf16)


def mid_kernel(xp, ob, vo0, vo1, gains, change, hmid, n2g):
    d = xp.shape[1]
    h = xp[...].astype(f32) + split_nt(ob[...], (vo0, vo1), slice(d, 2 * d))
    hmid[...] = h
    r2 = lax.rsqrt(jnp.mean(h * h, axis=-1, keepdims=True) + EPS)
    n2g[...] = nn((h * r2 * gains[1:2]).astype(bf16), change[...]).astype(bf16)


def ff_kernel(*refs):
    pieces, (wg, wu, *wd), (act, dg, du, keep, send, n2, gb, acc) = refs[:8], refs[8:12], refs[12:]
    rows = pieces[0].shape[0]
    for i in range(4):
        n2[i * rows : (i + 1) * rows] = pieces[i][...]
        gb[i * rows : (i + 1) * rows] = pieces[4 + i][...]
    half = n2.shape[0] // 2
    fc = wd[0].shape[1]
    for c in range(2):
        cols = slice(c * fc, (c + 1) * fc)
        gate = nn(n2[...], wg[:, cols])
        up = nn(n2[...], wu[:, cols])
        dact = nn(gb[...], wd[c][...])
        sig = jax.nn.sigmoid(gate)
        silu = gate * sig
        act[:, cols] = (silu * up).astype(bf16)
        dg[:, cols] = (dact * up * sig * (1.0 + gate * (1.0 - sig))).astype(bf16)
        du[:, cols] = (dact * silu).astype(bf16)
        part = nt(dg[:, cols], wg[:, cols]) + nt(du[:, cols], wu[:, cols])
        acc[...] = part if c == 0 else acc[...] + part
    keep[...] = acc[:half].astype(bf16)
    send[...] = acc[half:].astype(bf16)


def ff_grad_kernel(*refs):
    pieces, (act, dg, du), sides, (n2t, gbt) = refs[:8], refs[8:11], refs[11:-2], refs[-2:]
    rows = pieces[0].shape[0]
    for i in range(4):
        n2t[:, i * rows : (i + 1) * rows] = pieces[i][...].T
        gbt[:, i * rows : (i + 1) * rows] = pieces[4 + i][...].T
    fc = act.shape[1] // 2
    for c, (left, right) in enumerate(((n2t, dg[...]), (n2t, du[...]), (gbt, act[:, :fc]), (gbt, act[:, fc:]))):
        keep, send = sides[2 * c : 2 * c + 2]
        runs = 1 + c % 2
        run = n2t.shape[0] // (2 * runs)
        dw = nn(left[...], right).astype(bf16)
        for r in range(runs):
            keep[r * run : (r + 1) * run] = dw[2 * r * run : (2 * r + 1) * run]
            send[r * run : (r + 1) * run] = dw[(2 * r + 1) * run : (2 * r + 2) * run]


def ff_out_kernel(act, w0, w1, keep, send):
    half = act.shape[0] // 2
    fc = w0.shape[1]
    for ref, rows in ((keep, slice(0, half)), (send, slice(half, 2 * half))):
        ref[...] = (nt(act[rows, :fc], w0[...]) + nt(act[rows, fc:], w1[...])).astype(bf16)


def back_kernel(k1, g1, g2, hmid, gb, gains, vo0, vo1, ob, change, dh, dob, keep, send, dgain):
    t, d = hmid.shape
    half = d // 2
    total = k1[:t].astype(f32) + g1[:t].astype(f32) + g2[...].astype(f32)
    dn2 = moved(nt, total, change[...])
    h = hmid[...]
    r2 = lax.rsqrt(jnp.mean(h * h, axis=-1, keepdims=True) + EPS)
    dgain[...] = jnp.broadcast_to(jnp.sum(dn2 * h * r2, axis=0, keepdims=True), dgain.shape)
    dn2 = dn2 * gains[1:2]
    out = gb[...].astype(f32) + r2 * dn2 - h * (r2 * r2 * r2) * jnp.mean(dn2 * h, axis=-1, keepdims=True)
    dh[...] = out
    dob[...] = split_nn(out.astype(bf16), (vo0, vo1), slice(d, 2 * d)).astype(bf16)
    dw = nn(out.T.astype(bf16), ob[...]).astype(bf16)
    keep[...] = dw[:half]
    send[...] = dw[half:]


def attn_back_kernel(qr, kr, vb, dob, probs, n1t, cos, sin, seq_row, dq, dk, dv, keep, send):
    t, d = qr.shape
    half = d // 2
    pair = 2 * HD
    allowed = allowed_of(seq_row)
    low = lax.broadcasted_iota(jnp.int32, (t, pair), 1) < HD
    scale = HD ** -0.5
    for b in range(d // pair):
        cols = slice(b * pair, (b + 1) * pair)
        q, k, v, do = qr[:, cols], kr[:, cols], vb[:, cols], dob[:, cols]
        dqs, dks, dvs = [], [], []
        for h, mine in enumerate((low, ~low)):
            p = probs[2 * b + h]
            dp = nt(jnp.where(mine, do, jnp.zeros_like(do)), v)
            dlogit = p * (dp - jnp.sum(dp * p, axis=-1, keepdims=True))
            ds = jnp.where(allowed, dlogit * scale, 0.0)
            dvs.append(nn(p.T.astype(bf16), do))
            dqs.append(nn(ds.astype(bf16), k))
            dks.append(nn(ds.T.astype(bf16), q))
        dv[:, cols] = jnp.where(low, dvs[0], dvs[1]).astype(bf16)
        for grads, ref in ((dqs, dq), (dks, dk)):
            g = jnp.where(low, grads[0], grads[1])
            ref[:, cols] = (g * cos[...] - swap_halves(g) * sin[...]).astype(bf16)
    for part, ref in enumerate((dv, dq)):
        for b in range(d // 256):
            dw = nn(n1t[...], ref[:, b * 256 : (b + 1) * 256]).astype(bf16)
            cols = slice(part * d + b * 256, part * d + (b + 1) * 256)
            keep[:, cols] = dw[:half]
            send[:, cols] = dw[half:]


def last_kernel(dq, dk, dv, qk0, qk1, vo0, vo1, n1t, xp, dh, gains, dgain2, own_sel, dtok, keep, send):
    _, d = xp.shape
    half = d // 2
    qk, vo = (qk0, qk1), (vo0, vo1)
    dn1 = (split_nt(dq[...], qk, slice(0, d)) + split_nt(dk[...], qk, slice(d, 2 * d))
           + split_nt(dv[...], vo, slice(0, d)))
    dw = nn(n1t[...], dk[...]).astype(bf16)
    keep[:, :d] = dw[:half]
    send[:, :d] = dw[half:]
    x = xp[...].astype(f32)
    r1 = lax.rsqrt(jnp.mean(x * x, axis=-1, keepdims=True) + EPS)
    dgain1 = jnp.sum(dn1 * x * r1, axis=0, keepdims=True)
    row = lax.broadcasted_iota(jnp.int32, (128, d), 0)
    both = jnp.where(row == 0, dgain1, jnp.where(row == 1, dgain2[0:1], 0.0)).T.astype(bf16)
    keep[:, d:] = both[:half]
    send[:, d:] = both[half:]
    g = dn1 * gains[0:1]
    out = dh[...] + r1 * g - x * (r1 * r1 * r1) * jnp.mean(g * x, axis=-1, keepdims=True)
    dtok[...] = nt(out.astype(bf16), own_sel[...]).astype(bf16)


def out_kernel(k1, g1, g2, hmid, own_sel, group_sel, out):
    t = hmid.shape[0]
    total = k1[:t].astype(f32) + g1[:t].astype(f32) + g2[...].astype(f32)
    out[...] = (moved(nt, total, group_sel[...]) + moved(nt, hmid[...], own_sel[...])).astype(bf16)


def make_on_device(n):
    first, second = gather_orders(n)
    axis_bits = tuple(reversed(first))
    axis_of = {b: i for i, b in enumerate(axis_bits)}
    k = len(axis_bits)
    assert axis_bits[0] == first[-1] == second[-1]
    high = sorted((b for b in first if b not in LOW), reverse=True)
    ff_orders = (tuple(high), (high[-1],) + tuple(high[:-1]))
    ff_bits = tuple(reversed(high)) + tuple(reversed(LOW))
    ff_axis = {b: i for i, b in enumerate(ff_bits)}

    def swap(a, b):
        return lax.ppermute(a, "dp", [(i, i ^ b) for i in range(n)])

    def gather(shard, order):
        a = shard.reshape((1,) * k + shard.shape)
        for i, b in enumerate(order):
            got = swap(a, b)
            if i == k - 1:
                return tuple(v.reshape((n * shard.shape[0] // 2,) + shard.shape[1:]) for v in (a, got))
            a = jnp.concatenate([a, got], axis=axis_of[b])

    def reduce(keep, send, steps, axis, last):
        for i, b in enumerate(steps):
            got = swap(send, b)
            if i == len(steps) - 1:
                return (keep.astype(f32) + got.astype(f32)).astype(last) if last else (keep, got)
            ax = axis[steps[i + 1]]
            part = lambda v, at: lax.slice_in_dim(v, at, at + 1, axis=ax).astype(f32)
            send, keep = (
                (part(keep, 1) + part(got, 1)).astype(bf16),
                (part(keep, 0) + part(got, 0)).astype(bf16),
            )

    def scatter(keep, send, order):
        rows, cols = keep.shape[0] * 2 // n, keep.shape[1]
        shape = (1,) + (2,) * (k - 1) + (rows, cols)
        a = reduce(keep.reshape(shape), send.reshape(shape), tuple(reversed(order)), axis_of, f32)
        return a.reshape(rows, cols)

    def on_device(tokens, seq_ids, positions, cotangent, attn_gain, w_query, w_key, w_value, w_output,
                  mlp_gain, w_gate, w_up, w_down):
        toks, d = tokens.shape
        rows = d // n
        ff = w_gate.shape[1]
        share = 2 ** len(LOW)
        hidden = ff // share
        edges = cuts(hidden)
        widths = [b - a for a, b in zip(edges, edges[1:])]
        half = d // 2
        me = lax.axis_index("dp")

        def places_of(bits):
            slot = np.arange(d) // rows
            return sum(((slot >> (k - 1 - i)) & 1) * b for i, b in enumerate(bits)), np.arange(d) % rows

        places = jnp.asarray(np.stack([*places_of(axis_bits), *places_of(ff_bits), np.full(d, rows)]), jnp.int32)
        me1 = me[None]
        shards = [((rows, 2 * d + 128), bf16), ((rows, 2 * d), bf16)] + [((rows, 2 * ff * 3 // share), bf16)] * 2
        part_qk, part_vo, keep, send = call(
            pack_kernel, shards, me1, attn_gain[None, :], mlp_gain[None, :], w_query, w_key, w_value, w_output.T,
            w_gate, w_up, w_down.T, fetch=False, grant=3 * VMEM,
            scratch_shapes=[pltpu.VMEM((1, rows), bf16)] * 2 + [pltpu.SemaphoreType.DMA((18,))])
        mine = ff * 3 // share
        block = ((2, rows, mine), bf16)
        keep, send = call(fold_kernel, [block] * 2, me1, keep, swap(send, LOW[0]))
        ws = call(fold2_kernel, [((2, 2, rows, v), bf16) for v in widths], me1, keep, swap(send, LOW[1]))
        qk = gather(part_qk, first)
        vo = gather(part_vo, second)
        wff = []
        for c in range(PARTS):
            w = ws[c].reshape((1,) * len(high) + (2, 2, rows, widths[c]))
            for b in ff_orders[c % 2]:
                got = swap(w, b)
                w = jnp.concatenate([w, got], axis=ff_axis[b])
            wff.append(w.reshape(d, widths[c]))
        freq = jnp.exp(jnp.arange(HD // 2, dtype=f32) * (-2.0 * math.log(THETA) / HD))
        angles = positions.astype(f32)[:, None] * freq[None, :]
        cosine, sine = jnp.cos(angles), jnp.sin(angles)
        seq_row = seq_ids[None, :]
        act, mat, wide = ((toks, d), bf16), ((d, toks), bf16), ((toks, d), f32)

        def group_gather(v):
            far = swap(v, LOW[0])
            near = swap(v, LOW[1])
            return v, far, near, swap(far, LOW[1])

        def group_halve(keep, send):
            g1 = swap(send, LOW[1])
            v = (keep[toks:].astype(f32) + g1[toks:].astype(f32)).astype(bf16)
            return keep, g1, swap(v, LOW[0])

        square, table = ((d, d), bf16), ((toks, 2 * HD), f32)
        xp, gb, gbg, own_sel, group_sel, change, cos2, sin2 = call(
            prep_kernel, [act] * 3 + [square] * 3 + [table] * 2, me1, tokens, cotangent, places, seq_row, cosine, sine)
        gb4 = group_gather(gbg)
        n1t, qr, kr, vb, ob, probs, gains, _ = call(
            attn_kernel, [mat, act, act, act, act, ((H, toks, toks), f32), ((8, d), f32), act],
            xp, *qk, *vo, cos2, sin2, seq_row)
        hmid, n2g = call(mid_kernel, [wide, act], xp, ob, *vo, gains, change)
        n24 = group_gather(n2g)
        tg = share * toks
        pairs = [((tg // 2, d), bf16)] * 2
        acts, dg, du, keep, send = call(
            ff_kernel, [((tg, hidden), bf16)] * 3 + pairs, *n24, *gb4, *wff,
            scratch_shapes=[pltpu.VMEM((tg, d), bf16)] * 2 + [pltpu.VMEM((tg, d), f32)])
        dn2 = group_halve(keep, send)
        grads = call(
            ff_grad_kernel, [((half, v), bf16) for v in widths for _ in range(2)], *n24, *gb4, acts, dg, du,
            scratch_shapes=[pltpu.VMEM((d, tg), bf16)] * 2)
        y = group_halve(*call(ff_out_kernel, pairs, acts, *wff[2:]))
        parts = []
        for c in range(PARTS):
            steps = tuple(reversed(ff_orders[c % 2]))
            shape = tuple(1 if b == steps[0] else 2 for b in ff_bits) + (rows, widths[c])
            parts.append(reduce(*(v.reshape(shape) for v in grads[2 * c : 2 * c + 2]), steps, ff_axis, None))
        terms = [v.reshape(2, 2, rows, -1) for pair in parts for v in pair]
        keep, send = call(unfold_kernel, [block] * 2, me1, *terms)
        keep, send = call(unfold2_kernel, [block] * 2, me1, keep, swap(send, LOW[1]))
        got = swap(send, LOW[0])
        d_gate, d_up, d_down = call(
            unpack_kernel, [((rows, ff), f32)] * 3, me1, keep, got)
        dh, dob, keep, send, dgain2 = call(
            back_kernel, [wide, act, ((half, d), bf16), ((half, d), bf16), ((8, d), f32)],
            *dn2, hmid, gb, gains, *vo, ob, change)
        d_wo = scatter(keep, send, second)
        dq, dk, dv, keep, send = call(
            attn_back_kernel, [act, act, act, ((half, 2 * d), bf16), ((half, 2 * d), bf16)],
            qr, kr, vb, dob, probs, n1t, cos2, sin2, seq_row)
        d_vq = scatter(keep, send, first)
        dtok, keep, send = call(
            last_kernel, [act, ((half, d + 128), bf16), ((half, d + 128), bf16)],
            dq, dk, dv, *qk, *vo, n1t, xp, dh, gains, dgain2, own_sel)
        d_kg = scatter(keep, send, second)
        (out,) = call(out_kernel, [act], *y, hmid, own_sel, group_sel)
        gain_one, key, gain_two = d_kg[:, d], d_kg[:, :d], d_kg[:, d + 1]
        query, value = d_vq[:, d:], d_vq[:, :d]
        output = d_wo.T
        return (out, dtok, gain_one, query, key, value, output, gain_two, d_gate, d_up, d_down.T)

    return on_device


def solution(mesh):
    rows, cols, vec = P("dp", None), P(None, "dp"), P("dp")
    in_specs = (rows, vec, vec, rows, vec, rows, rows, rows, cols, vec, rows, rows, cols)
    out_specs = (rows, rows, vec, rows, rows, rows, cols, vec, rows, rows, cols)
    n = mesh.shape["dp"]
    return jax.shard_map(make_on_device(n), mesh=mesh, in_specs=in_specs, out_specs=out_specs, check_vma=False)
```
